512 devices in a mesh: seq: 16 (over x, y), exp: 32 (over z, core).
Axes of the slice: x: 4, y: 4, z: 16, core: 2. Of those that a mesh axis runs over, the one named last changes fastest.
Arguments:
- residual: bfloat16 [2048, 2, 3072], P(('seq', 'exp')), may hold values from -6 to 6
- queries: bfloat16 [2, 2048, 4096], P(None, 'seq', 'exp'), may hold values from -6 to 6
- key_vecs: bfloat16 [2, 2048, 4096], P(None, 'seq', 'exp'), may hold values from -0.52734375 to 0.52734375
- value_vecs: bfloat16 [2, 2048, 4096], P(None, 'seq', 'exp'), may hold values from -6 to 6
- log_decay: float32 [2, 32, 2048], P(None, 'exp', 'seq'), may hold values from -2 to 0
- head_gain: float32 [4096], P('exp'), may hold values from 0.1 to 1.9
- out_proj: bfloat16 [4096, 3072], P('exp'), may hold values from -0.09375 to 0.09375
- norm_gain: float32 [3072], replicated, may hold values from 0.1 to 1.9
- routes: int32 [2048, 2, 2], replicated, may hold values from 0 to 31, all different within a row; in each aligned block of 256 rows (0 to 255, 256 to 511, ..., all dimensions but the last counted through in order) at most 32 rows name the same one
- route_weight: float32 [2048, 2, 2], replicated, may hold values from 0.1 to 1
- w_gate: bfloat16 [32, 4608, 3072], P('exp', 'seq'), may hold values from -0.109375 to 0.109375
- w_up: bfloat16 [32, 4608, 3072], P('exp', 'seq'), may hold values from -0.109375 to 0.109375
Outputs:
- attn_out: float32 [2048, 2, 3072], P(('seq', 'exp'))
- expert_hidden: float32 [32, 4608, 512], P('exp', 'seq')
The draws below stay inside these ranges and needn't reach their ends.
Inputs may be any that keep to these rules, and one draw needn't show every extreme that they name: Each aligned block of 256 rows of routes (positions c * 128 .. (c + 1) * 128 - 1 of both sequences) names one expert at most 32 times, a bound that some block reaches; the 2 entries of a row differ.
All inputs are finite; a program needn't handle non-finite values.
Results may differ from the reference program's by a relative error of at most 0.0052.
Values may be sent and summed in bfloat16 or wider, within the bound.
A program may use at most 64 MiB of HBM per device.

```python
import math
import jax
import jax.numpy as jnp
import numpy as np
from jax import lax

D = 3072
ATTN_GROUPS = 32
HS = 128
FF = 4608
TOPK = 2
BATCH_SIZE = 2
LC = 128
TOKEN_SPAN = 2048
EXPERTS = 32
RCAP = 32


def draw_log_decay(key, part):
    whole_tuple = jax.random.split(key, 7)
    head_shape = (1, ATTN_GROUPS, 1)
    fast_flag = jax.random.randint(whole_tuple[0], head_shape, 0, 2) == 0
    slow_rate = jnp.exp(jax.random.uniform(whole_tuple[1], head_shape, minval=jnp.log(0.05), maxval=jnp.log(0.4))) / TOKEN_SPAN
    fast_rate = jnp.exp(jax.random.uniform(whole_tuple[2], head_shape, minval=jnp.log(1.0 / 50.0), maxval=jnp.log(1.0 / 30.0)))
    nominal_speed = jnp.where(fast_flag, fast_rate, slow_rate)
    processor_factor = jnp.exp(jax.random.uniform(whole_tuple[3], (BATCH_SIZE, ATTN_GROUPS, TOKEN_SPAN // LC), minval=jnp.log(0.6), maxval=jnp.log(1.7)))
    processor_factor = jnp.repeat(processor_factor, LC, axis=2)
    locus_scaling = jax.random.uniform(whole_tuple[4], (BATCH_SIZE, ATTN_GROUPS, TOKEN_SPAN), minval=0.5, maxval=1.5)
    spike_location = jax.random.randint(whole_tuple[5], (BATCH_SIZE, ATTN_GROUPS, 2), 0, TOKEN_SPAN)
    spike_slowdown = jax.random.uniform(whole_tuple[6], (BATCH_SIZE, ATTN_GROUPS, 2), minval=0.2, maxval=0.5)
    location_array = jnp.arange(TOKEN_SPAN, dtype=jnp.int32)
    spike_occurrences = jnp.sum(jnp.where(location_array[None, None, None, :] == spike_location[..., None], jnp.log(1.0 - spike_slowdown)[..., None], 0.0), axis=2)
    return (-nominal_speed * processor_factor * locus_scaling + spike_occurrences).astype(jnp.float32)


def steps_of(key, shape, cuts, smallest, largest):
    gain = 1.0
    for position, shards_of in cuts:
        heights = jax.random.uniform(jax.random.fold_in(jax.random.fold_in(key, 6), position), (shards_of,), jnp.float32, smallest / len(cuts), largest / len(cuts))
        gain = gain * jnp.repeat(jnp.exp(heights), shape[position] // shards_of).reshape((-1,) + (1,) * (len(shape) - 1 - position))
    return gain


def routed_block(key, own, number, rows, number_of, top, most, slope):
    sequence = jax.random.permutation(key, number_of)
    heavy_load, ordinary = portions_of(number_of, rows * top, most, slope, True), portions_of(number_of, rows * top, most, slope, False)
    places = jnp.arange(number_of)

    def named(tallies, turn):
        used = int((tallies > 0).sum())
        fixed = max(1, used // 4)
        moved = fixed + (places - fixed + turn * (used - fixed)) % max(1, number_of - fixed)
        return jnp.zeros((number_of,), jnp.int32).at[sequence[jnp.where(places < fixed, places, moved)]].set(jnp.asarray(tallies, jnp.int32))

    tallies = jnp.where(number % 4 == 0, named(heavy_load, number // 4), named(ordinary, number - number // 4 - 1))
    mixed = jax.random.permutation(jax.random.fold_in(own, 3), number_of)
    donor, taker = mixed[0:number_of // 2 * 2:2], mixed[1:number_of // 2 * 2:2]
    margin = jnp.minimum(tallies[donor] - 1, most - tallies[taker]) // 2
    margin = jnp.where((donor == sequence[0]) | (taker == sequence[0]) | (tallies[taker] == 0), 0, jnp.maximum(margin, 0))
    moved = jax.random.randint(jax.random.fold_in(own, 4), (number_of // 2,), 0, 1 << 20) % (margin + 1)
    tallies = tallies.at[donor].add(-moved).at[taker].add(moved)
    labels = jnp.searchsorted(jnp.cumsum(tallies), jnp.arange(rows * top), side="right").astype(jnp.int32)
    listing = labels.reshape(top, rows).T
    listing = listing[jax.random.permutation(jax.random.fold_in(own, 1), rows)]
    turn = jax.random.randint(jax.random.fold_in(own, 2), (rows, 1), 0, top)
    return jnp.take_along_axis(listing, (jnp.arange(top)[None, :] + turn) % top, axis=1)


def portions_of(count, total, bound, lean, full):
    loads = [(1 << 20) // math.isqrt(rank ** lean) + 1 for rank in range(1, count + 1)]
    largest = bound if full else min(bound, max(-(-total // count), total * loads[0] // sum(loads)))
    least = 1 if total - largest >= count - 1 else 0
    holding, surplus = [largest] + [least] * (count - 1), total - largest - least * (count - 1)
    while surplus > 0:
        movable = [i for i in range(1, count) if holding[i] < largest] or [i for i in range(1, count) if holding[i] < bound]
        whole, remaining = sum([loads[i] for i in movable]), surplus
        for i in movable:
            addition = min(bound - holding[i], max(1, remaining * loads[i] // whole), surplus)
            holding[i] = holding[i] + addition
            surplus = surplus - addition
    return np.array(holding)


def noise(own_key, dims, spread, reach, cuts=(), kind=jnp.bfloat16):
    drawn = jax.random.normal(own_key, dims, jnp.float32) * spread
    if len(cuts) > 0:
        drawn = steps_of(own_key, dims, cuts, -0.22, 0.18) * drawn
    return jnp.clip(drawn, min=-reach, max=reach).astype(kind)


def setup_inputs(seed: int = 0) -> dict:
    seeds = jax.random.split(jax.random.key(seed), 13)
    residual = noise(seeds[0], (TOKEN_SPAN, BATCH_SIZE, D), 1.0, 6.0, ((0, 512),))
    queries = noise(seeds[1], (BATCH_SIZE, TOKEN_SPAN, ATTN_GROUPS * HS), 1.0, 6.0, ((1, 16), (2, 32)))
    key_vecs = noise(seeds[2], (BATCH_SIZE, TOKEN_SPAN, ATTN_GROUPS * HS), 0.088, 0.52734375, ((1, 16), (2, 32)))
    value_vecs = noise(seeds[3], (BATCH_SIZE, TOKEN_SPAN, ATTN_GROUPS * HS), 1.0, 6.0, ((1, 16), (2, 32)))
    log_decay = draw_log_decay(jax.random.fold_in(seeds[12], 71), 0)
    head_gain = jnp.clip(1.0 + 0.18 * jax.random.normal(seeds[5], (ATTN_GROUPS * HS,), jnp.float32), 0.1, 1.9)
    out_proj = noise(seeds[6], (ATTN_GROUPS * HS, D), (ATTN_GROUPS * HS) ** -0.5, 0.09375, ((0, 32),))
    norm_gain = jnp.clip(1.0 + 0.18 * jax.random.normal(seeds[7], (D,), jnp.float32), 0.1, 1.9)
    routes_keys = jax.random.split(jax.random.fold_in(seeds[8], 1), TOKEN_SPAN * BATCH_SIZE // (2 * LC))
    routes_turns = jax.random.permutation(jax.random.fold_in(seeds[8], 3), TOKEN_SPAN * BATCH_SIZE // (2 * LC))
    routes = jax.vmap(lambda own, number: routed_block(jax.random.fold_in(seeds[8], 2), own, number, 2 * LC, EXPERTS, TOPK, RCAP, 2))(routes_keys, routes_turns).reshape((TOKEN_SPAN, BATCH_SIZE, TOPK))
    route_weight = jnp.clip(jax.random.uniform(seeds[9], (TOKEN_SPAN, BATCH_SIZE, TOPK), jnp.float32, 0.1, 1.0), 0.1, 1.0)
    w_gate = noise(seeds[10], (EXPERTS, FF, D), D ** -0.5, 0.109375, ((0, 32), (1, 16)))
    w_up = noise(seeds[11], (EXPERTS, FF, D), D ** -0.5, 0.109375, ((0, 32), (1, 16)))
    return {"residual": residual, "queries": queries, "key_vecs": key_vecs, "value_vecs": value_vecs, "log_decay": log_decay, "head_gain": head_gain, "out_proj": out_proj, "norm_gain": norm_gain, "routes": routes, "route_weight": route_weight, "w_gate": w_gate, "w_up": w_up}


PRECISE = lax.Precision.HIGHEST

def row_norm(values_in, gain_vec):
    meansq = lax.optimization_barrier(jnp.mean(values_in * values_in, axis=-1, keepdims=True))
    return values_in * lax.rsqrt(meansq + 1e-06) * gain_vec

def blocks_of(array_in):
    return array_in.astype(jnp.float32).reshape(BATCH_SIZE, TOKEN_SPAN // LC, LC, ATTN_GROUPS, HS).transpose(1, 0, 3, 2, 4)

def reference(residual, queries, key_vecs, value_vecs, log_decay, head_gain, out_proj, norm_gain, routes, route_weight, w_gate, w_up):
    query_b = blocks_of(queries)
    key_b = blocks_of(key_vecs)
    value_b = blocks_of(value_vecs)
    decay_b = log_decay.reshape(BATCH_SIZE, ATTN_GROUPS, TOKEN_SPAN // LC, LC).transpose(2, 0, 1, 3)
    causal_mask = jnp.tril(jnp.ones((LC, LC), dtype=bool))

    def advance(state_now, block_data):
        query_t, key_t, value_t, decay_t = block_data
        running = jnp.cumsum(decay_t, axis=-1)
        spread_log = running[..., :, None] - running[..., None, :]
        decay_mat = jnp.where(causal_mask, jnp.exp(jnp.where(causal_mask, spread_log, 0.0)), 0.0)
        scores = jnp.einsum('bhtc,bhjc->bhtj', query_t, key_t, precision=PRECISE) * decay_mat
        inner_part = jnp.einsum('bhtj,bhjd->bhtd', scores, value_t, precision=PRECISE)
        outer_part = jnp.exp(running)[..., None] * jnp.einsum('bhtc,bhcd->bhtd', query_t, state_now, precision=PRECISE)
        tail_decay = jnp.exp(running[..., -1:] - running)
        fresh_state = jnp.einsum('bhjc,bhjd->bhcd', key_t * tail_decay[..., None], value_t, precision=PRECISE)
        state_now = jnp.exp(running[..., -1])[..., None, None] * state_now + fresh_state
        return (state_now, inner_part + outer_part)
    start_state = jnp.zeros((BATCH_SIZE, ATTN_GROUPS, HS, HS), jnp.float32)
    final_state, outputs = lax.scan(advance, start_state, (query_b, key_b, value_b, decay_b))
    normed_heads = row_norm(outputs, head_gain.reshape(ATTN_GROUPS, HS)[None, None, :, None, :])
    attention = normed_heads.transpose(0, 3, 1, 2, 4).reshape(TOKEN_SPAN, BATCH_SIZE, ATTN_GROUPS * HS).astype(jnp.bfloat16)
    projected = jnp.dot(attention.reshape(TOKEN_SPAN * BATCH_SIZE, ATTN_GROUPS * HS), out_proj, preferred_element_type=jnp.float32).reshape(TOKEN_SPAN, BATCH_SIZE, D)
    mixed_rows = residual.astype(jnp.float32) + projected
    attn_out = mixed_rows
    normed = row_norm(mixed_rows, norm_gain).astype(jnp.bfloat16)
    row_count = 2 * LC
    groups = normed.astype(jnp.float32).reshape(TOKEN_SPAN // LC, row_count, D)
    route_blocks = routes.reshape(TOKEN_SPAN // LC, row_count, TOPK)
    weight_blocks = route_weight.reshape(TOKEN_SPAN // LC, row_count, TOPK)
    slot_ids = jnp.arange(RCAP, dtype=jnp.int32)

    def per_expert(expert_id):
        route_hits = route_blocks == expert_id
        chosen = jnp.any(route_hits, axis=-1)
        token_weight = lax.optimization_barrier(jnp.sum(jnp.where(route_hits, weight_blocks, 0.0), axis=-1))
        slot_rank = jnp.cumsum(chosen.astype(jnp.int32), axis=1) - 1
        pick_table = ((slot_rank[:, None, :] == slot_ids[None, :, None]) & chosen[:, None, :]).astype(jnp.float32)
        slot_weight = jnp.einsum('csj,cj->cs', pick_table, token_weight, precision=PRECISE).reshape(-1)
        slot_rows = jnp.einsum('csj,cjd->csd', pick_table, groups, precision=PRECISE).astype(jnp.bfloat16).reshape(-1, D)
        gate_val = lax.dot_general(w_gate[expert_id], slot_rows, (((1,), (1,)), ((), ())), preferred_element_type=jnp.float32)
        up_val = lax.dot_general(w_up[expert_id], slot_rows, (((1,), (1,)), ((), ())), preferred_element_type=jnp.float32)
        return slot_weight[None, :] * jax.nn.silu(gate_val) * up_val
    expert_hidden = lax.map(per_expert, jnp.arange(EXPERTS, dtype=jnp.int32))
    return (attn_out, expert_hidden)
```

```python
import functools

import jax
import jax.numpy as jnp
from jax import lax
from jax.experimental import pallas as pl
from jax.experimental.pallas import tpu as pltpu
from jax.sharding import PartitionSpec as P

MESH = pl.DeviceIdType.MESH
BF = jnp.bfloat16
F32 = jnp.float32
SIDE = 4
CHIPS = 16
LC = 128
HS = 128
SLOTS = 32
ST = 2 * HS + 8


def dot(a, b, dims):
    return lax.dot_general(a, b, (dims, ((), ())), preferred_element_type=F32)


NN = ((1,), (0,))
NT = ((1,), (1,))
TN = ((0,), (0,))


def split(a):
    hi = a.astype(BF)
    return hi, (a - hi.astype(F32)).astype(BF)


def remote(src, dst, send, recv, peer):
    return pltpu.make_async_remote_copy(
        src, dst, send, recv, device_id=peer, device_id_type=MESH
    )


def kernel(
    q_ref,
    k_ref,
    v_ref,
    ld_ref,
    hg_ref,
    res_ref,
    outp_ref,
    ng_ref,
    rt_ref,
    wt_ref,
    wg_ref,
    wu_ref,
    attn_ref,
    hid_ref,
    ybuf,
    xbuf,
    prefix,
    inc,
    inner,
    grow,
    att,
    w2,
    part,
    own,
    rsbuf,
    resbuf,
    res16,
    mix,
    nrm,
    rts,
    wts,
    picks,
    slots,
    other,
    sw,
    wgb,
    wub,
    lsem,
    ysend,
    yrecv,
    xsend,
    xrecv,
    bsend,
    brecv,
    zsend,
    zrecv,
    gsend,
    grecv,
    ssend,
    srecv,
):
    s = lax.axis_index("seq")
    e = lax.axis_index("exp")
    x, y, z, c = s // SIDE, s % SIDE, e // 2, e % 2
    half = mix.shape[2]
    depth = 2 * half

    def at(xx, yy, zz, cc):
        return (xx * SIDE + yy, zz * 2 + cc)

    sib = at(x, y, z, 1 - c)
    barrier = pltpu.get_barrier_semaphore()

    def greet(peer):
        pl.semaphore_signal(barrier, inc=1, device_id=peer, device_id_type=MESH)

    greet(sib)
    for d in range(1, SIDE):
        greet(at(x, (y + d) % SIDE, z, c))
        greet(at((x + d) % SIDE, y, z, c))

    def greet_z(d, _):
        greet(at(x, y, (z + d) % CHIPS, c))
        return 0

    lax.fori_loop(1, CHIPS, greet_z, 0)

    mine = pl.ds(pl.multiple_of(c * half, half), half)
    theirs = pl.ds(pl.multiple_of((1 - c) * half, half), half)
    own_k = pl.ds(pl.multiple_of(c * HS, HS), HS)
    w2_own = pltpu.make_async_copy(outp_ref.at[:, mine], w2.at[own_k, :], lsem.at[0])
    wg_copy = pltpu.make_async_copy(wg_ref.at[0], wgb, lsem.at[1])
    wu_copy = pltpu.make_async_copy(wu_ref.at[0], wub, lsem.at[2])
    w2_own.start()
    wg_copy.start()
    wu_copy.start()

    ti = lax.broadcasted_iota(jnp.int32, (LC, LC), 0)
    ji = lax.broadcasted_iota(jnp.int32, (LC, LC), 1)
    causal = ji <= ti
    run_cols, run_rows = [], []
    for b in range(2):
        lb = jnp.broadcast_to(ld_ref[b], (LC, LC))
        rc = jnp.sum(jnp.where(causal, lb, 0.0), axis=1, keepdims=True)
        rr = jnp.sum(jnp.where(ji == ti, rc, 0.0), axis=0, keepdims=True)
        run_cols.append(rc)
        run_rows.append(rr)
        total = rr[:, LC - 1 :]
        kw = k_ref[b].astype(F32) * jnp.exp(total - rc)
        hi, lo = split(kw)
        vb = v_ref[b]
        ybuf[y, pl.ds(b * HS, HS), :] = dot(hi, vb, TN) + dot(lo, vb, TN)
        ybuf[y, pl.ds(2 * HS + b, 1), :] = jnp.broadcast_to(total, (1, HS))
    ybuf[y, pl.ds(2 * HS + 2, 6), :] = jnp.zeros((6, HS), F32)

    pl.semaphore_wait(barrier, 2 * (SIDE - 1) + CHIPS)

    ycopies = []
    for d in range(1, SIDE):
        cp = remote(
            ybuf.at[y], ybuf.at[y], ysend.at[d], yrecv.at[y], at(x, (y + d) % SIDE, z, c)
        )
        cp.start()
        ycopies.append(cp)
    w2_sib = remote(outp_ref.at[:, theirs], w2.at[own_k, :], bsend.at[0], brecv.at[0], sib)
    w2_sib.start()
    res_sib = remote(res_ref, resbuf.at[c], bsend.at[1], brecv.at[1], sib)
    res_sib.start()
    resbuf[c] = res_ref[...]

    for b in range(2):
        rc, rr = run_cols[b], run_rows[b]
        decay = jnp.where(causal, jnp.exp(jnp.where(causal, rc - rr, 0.0)), 0.0)
        hi, lo = split(dot(q_ref[b], k_ref[b], NT) * decay)
        vb = v_ref[b]
        inner[b] = dot(hi, vb, NN) + dot(lo, vb, NN)
        grow[b] = jnp.broadcast_to(jnp.exp(rc), (LC, HS))

    for d in range(1, SIDE):
        yy = (y + d) % SIDE
        remote(
            ybuf.at[yy], ybuf.at[yy], ysend.at[d], yrecv.at[yy], at(x, yy, z, c)
        ).wait_recv()
    for b in range(2):
        rows = pl.ds(b * HS, HS)
        run = jnp.zeros((HS, HS), F32)
        logs = jnp.zeros((1, HS), F32)
        pre = jnp.zeros((HS, HS), F32)
        prelog = jnp.zeros((1, HS), F32)
        for i in range(SIDE):
            pre = jnp.where(y == i, run, pre)
            prelog = jnp.where(y == i, logs, prelog)
            tot = ybuf[i, pl.ds(2 * HS + b, 1), :]
            run = jnp.exp(tot) * run + ybuf[i, rows, :]
            logs = logs + tot
        prefix[rows, :] = pre
        prefix[pl.ds(2 * HS + b, 1), :] = prelog
        xbuf[x, rows, :] = run
        xbuf[x, pl.ds(2 * HS + b, 1), :] = logs
    xbuf[x, pl.ds(2 * HS + 2, 6), :] = jnp.zeros((6, HS), F32)
    for d in range(1, SIDE):

        @pl.when(x + d < SIDE)
        def _():
            remote(
                xbuf.at[x], xbuf.at[x], xsend.at[d], xrecv.at[x], at((x + d) % SIDE, y, z, c)
            ).start()

    for b in range(2):
        for kk in range(2):
            for blk in range(CHIPS):
                cols = pl.ds(blk * LC, LC)
                rts[b * 2 + kk, pl.ds(blk, 1), :] = rt_ref[b, pl.ds(kk, 1), cols]
                wts[b * 2 + kk, pl.ds(blk, 1), :] = wt_ref[b, pl.ds(kk, 1), cols]
    before = (ti < ji).astype(F32).astype(BF)
    slot_id = lax.broadcasted_iota(jnp.int32, (SLOTS, LC), 0).astype(F32)
    ri = lax.broadcasted_iota(jnp.int32, (2 * LC, 2 * LC), 0)
    ci = lax.broadcasted_iota(jnp.int32, (2 * LC, 2 * LC), 1)
    rb, rtm = ri // LC, ri % LC
    perm = (ci == (rtm // 8) * 16 + rb * 8 + rtm % 8).astype(F32).astype(BF)

    def places(h0, h1):
        first = dot((h0 + h1).astype(BF), before, NN)
        return first, first + h0

    for ex in range(2):
        hits = []
        for b in range(2):
            r0 = rts[b * 2, pl.ds(s, 1), :]
            r1 = rts[b * 2 + 1, pl.ds(s, 1), :]
            hit = ((r0 == z * 2 + ex) | (r1 == z * 2 + ex)).astype(F32)
            hits.append(jnp.broadcast_to(hit, (8, LC)))
        p0, p1 = places(hits[0], hits[1])
        table = []
        for hh, pp in ((hits[0], p0), (hits[1], p1)):
            one = jnp.where(slot_id == pp[0:1, :], hh[0:1, :], 0.0)
            table.append(one)
        table = jnp.concatenate(table, axis=1).astype(BF)
        picks[pl.ds(ex * SLOTS, SLOTS), :] = dot(table, perm, NN).astype(BF)

    hits = [((rts[b * 2] == e) | (rts[b * 2 + 1] == e)).astype(F32) for b in range(2)]
    tws = [
        jnp.where(rts[b * 2] == e, wts[b * 2], 0.0)
        + jnp.where(rts[b * 2 + 1] == e, wts[b * 2 + 1], 0.0)
        for b in range(2)
    ]
    ranks = places(hits[0], hits[1])
    for blk in range(CHIPS):
        acc = jnp.zeros((8, SLOTS), F32)
        for b in range(2):
            row = slice(blk, blk + 1)
            one = jnp.where(slot_id == ranks[b][row], hits[b][row], 0.0).astype(BF)
            w = jnp.broadcast_to(tws[b][row], (8, LC))
            hi = w.astype(BF)
            rest = w - hi.astype(F32)
            mid, low = split(rest)
            acc = acc + (dot(hi, one, NT) + (dot(mid, one, NT) + dot(low, one, NT)))
        sw[:, pl.ds(blk * SLOTS, SLOTS)] = acc

    inc[...] = jnp.zeros_like(inc)
    for i in range(SIDE - 1):

        @pl.when(x > i)
        def _():
            remote(
                xbuf.at[i], xbuf.at[i], xsend.at[0], xrecv.at[i], at(i, y, z, c)
            ).wait_recv()
            for b in range(2):
                rows = pl.ds(b * HS, HS)
                tot = xbuf[i, pl.ds(2 * HS + b, 1), :]
                inc[rows, :] = jnp.exp(tot) * inc[rows, :] + xbuf[i, rows, :]

    heads = []
    for b in range(2):
        rows = pl.ds(b * HS, HS)
        state = prefix[rows, :] + jnp.exp(prefix[pl.ds(2 * HS + b, 1), :]) * inc[rows, :]
        hi, lo = split(state)
        qb = q_ref[b]
        raw = inner[b] + grow[b] * (dot(qb, hi, NN) + dot(qb, lo, NN))
        meansq = jnp.mean(raw * raw, axis=1, keepdims=True)
        heads.append((raw * lax.rsqrt(meansq + 1e-06) * hg_ref[...]).reshape(CHIPS, 1, 8, HS))
    att[:, own_k] = jnp.concatenate(heads, axis=1).reshape(2 * LC, HS).astype(BF)
    att_sib = remote(att.at[:, own_k], att.at[:, own_k], bsend.at[2], brecv.at[2], sib)
    att_sib.start()

    w2_own.wait()
    other_k = pl.ds(pl.multiple_of((1 - c) * HS, HS), HS)
    remote(outp_ref.at[:, theirs], w2.at[other_k, :], bsend.at[0], brecv.at[0], sib).wait_recv()
    remote(att.at[:, own_k], att.at[:, other_k], bsend.at[2], brecv.at[2], sib).wait_recv()
    own_rows = pl.ds(pl.multiple_of(z * 16, 16), 16)
    for j in range(half // 256):
        cols = pl.ds(j * 256, 256)
        part[:, cols] = dot(att[...], w2[:, cols], NN).astype(BF)
    own[...] = dot(att[own_rows, :], w2[...], NN)

    def far_first(i):
        return CHIPS // 2 + ((i + 1) // 2) * (1 - 2 * (i % 2))

    def send_part(i, _):
        zz = (z + far_first(i)) % CHIPS
        rows = pl.ds(pl.multiple_of(zz * 16, 16), 16)
        remote(
            part.at[rows, :], rsbuf.at[own_rows, :], zsend.at[zz], zrecv.at[z], at(x, y, zz, c)
        ).start()
        return 0

    lax.fori_loop(0, CHIPS - 1, send_part, 0)

    remote(res_ref, resbuf.at[1 - c], bsend.at[1], brecv.at[1], sib).wait_recv()
    for cc in range(2):
        for i in range(4):
            two = resbuf[cc, i, :, mine].astype(F32)
            for b in range(2):
                res16[pl.ds(b * 8 + cc * 4 + i, 1), :] = two[b : b + 1, :]

    def wait_part(d, _):
        zz = (z + d) % CHIPS
        rows = pl.ds(pl.multiple_of(zz * 16, 16), 16)
        remote(
            part.at[rows, :], rsbuf.at[rows, :], zsend.at[zz], zrecv.at[zz], at(x, y, zz, c)
        ).wait_recv()
        return 0

    lax.fori_loop(1, CHIPS, wait_part, 0)
    acc = own[...] + res16[...]
    for d in range(1, CHIPS):
        rows = pl.ds(pl.multiple_of(((z + d) % CHIPS) * 16, 16), 16)
        acc = acc + rsbuf[rows, :].astype(F32)
    mix[c] = acc
    mix_sib = remote(mix.at[c], mix.at[c], bsend.at[3], brecv.at[3], sib)
    mix_sib.start()
    ss = jnp.sum(acc * acc, axis=1, keepdims=True)
    remote(mix.at[c], mix.at[1 - c], bsend.at[3], brecv.at[3], sib).wait_recv()
    far = mix[1 - c]
    ss = ss + jnp.sum(far * far, axis=1, keepdims=True)
    scale = lax.rsqrt(ss * (1.0 / depth) + 1e-06)
    nrm[own_rows, :] = (mix[c] * scale * ng_ref[:, mine]).astype(BF)

    def send_norm(i, _):
        zz = (z + far_first(i)) % CHIPS
        remote(
            nrm.at[own_rows, :], nrm.at[own_rows, :], gsend.at[zz], grecv.at[z], at(x, y, zz, c)
        ).start()
        return 0

    lax.fori_loop(0, CHIPS - 1, send_norm, 0)
    for h in range(2):
        for b in range(2):
            for i in range(4):
                attn_ref[i, pl.ds(b, 1), pl.ds(h * half, half)] = mix[
                    h, pl.ds(b * 8 + c * 4 + i, 1), :
                ]

    def wait_norm(d, _):
        zz = (z + d) % CHIPS
        rows = pl.ds(pl.multiple_of(zz * 16, 16), 16)
        remote(
            nrm.at[rows, :], nrm.at[rows, :], gsend.at[zz], grecv.at[zz], at(x, y, zz, c)
        ).wait_recv()
        return 0

    lax.fori_loop(1, CHIPS, wait_norm, 0)

    blk_rows = pl.ds(pl.multiple_of(s * SLOTS, SLOTS), SLOTS)
    theirs_p = pl.ds(pl.multiple_of((1 - c) * SLOTS, SLOTS), SLOTS)
    mine_p = pl.ds(pl.multiple_of(c * SLOTS, SLOTS), SLOTS)
    other[...] = dot(picks[theirs_p, :], nrm[...], NN).astype(BF)
    pick_sib = remote(other, slots.at[c, blk_rows, :], bsend.at[4], brecv.at[4], sib)
    pick_sib.start()
    slots[c, blk_rows, :] = dot(picks[mine_p, :], nrm[...], NN).astype(BF)
    remote(other, slots.at[1 - c, blk_rows, :], bsend.at[4], brecv.at[4], sib).wait_recv()

    def piece(h, bx, by, sem, peer):
        blk = bx * SIDE + by
        rows = pl.ds(pl.multiple_of(blk * SLOTS, SLOTS), SLOTS)
        ref = slots.at[h, rows, :]
        return remote(ref, ref, ssend.at[h, sem], srecv.at[h, blk], peer)

    for d in range(1, SIDE):
        piece(0, x, y, d, at((x + d) % SIDE, y, z, c)).start()
        piece(1, x, y, d, at(x, (y + d) % SIDE, z, c)).start()
    for m in range(SIDE):
        xx, yy = (x + m) % SIDE, (y + m) % SIDE
        if m:
            piece(0, xx, y, 0, sib).wait_recv()
        for d in range(1, SIDE):
            piece(0, xx, y, SIDE * (m + 1) + d, at(x, (y + d) % SIDE, z, c)).start()
        if m:
            piece(1, x, yy, 0, sib).wait_recv()
        for d in range(1, SIDE):
            piece(1, x, yy, SIDE * (m + 1) + d, at((x + d) % SIDE, y, z, c)).start()
    for m in range(SIDE):
        xx, yy = (x + m) % SIDE, (y + m) % SIDE
        for d in range(1, SIDE):
            piece(0, xx, (y + d) % SIDE, 0, sib).wait_recv()
            piece(1, (x + d) % SIDE, yy, 0, sib).wait_recv()

    wg_copy.wait()
    wu_copy.wait()
    for n in range(2):
        rows = pl.ds(n * 256, 256)
        gate = dot(wgb[:, :half], slots[0, rows, :], NT) + dot(wgb[:, half:], slots[1, rows, :], NT)
        up = dot(wub[:, :half], slots[0, rows, :], NT) + dot(wub[:, half:], slots[1, rows, :], NT)
        hid_ref[0, :, rows] = sw[0:1, rows] * (gate / (1.0 + jnp.exp(-gate))) * up

    for cp in ycopies:
        cp.wait_send()
    for d in range(1, SIDE):

        @pl.when(x + d < SIDE)
        def _():
            remote(
                xbuf.at[x], xbuf.at[x], xsend.at[d], xrecv.at[x], at((x + d) % SIDE, y, z, c)
            ).wait_send()

    for cp in (w2_sib, res_sib, att_sib, mix_sib, pick_sib):
        cp.wait_send()

    def drain(d, _):
        zz = (z + d) % CHIPS
        rows = pl.ds(pl.multiple_of(zz * 16, 16), 16)
        peer = at(x, y, zz, c)
        remote(part.at[rows, :], rsbuf.at[own_rows, :], zsend.at[zz], zrecv.at[z], peer).wait_send()
        remote(
            nrm.at[own_rows, :], nrm.at[own_rows, :], gsend.at[zz], grecv.at[z], peer
        ).wait_send()
        return 0

    lax.fori_loop(1, CHIPS, drain, 0)
    for h in range(2):
        for m in range(SIDE + 1):
            for d in range(1, SIDE):
                piece(h, x, y, SIDE * m + d, sib).wait_send()


def per_device(
    residual,
    queries,
    key_vecs,
    value_vecs,
    log_decay,
    head_gain,
    out_proj,
    norm_gain,
    routes,
    route_weight,
    w_gate,
    w_up,
):
    model_width = residual.shape[2]
    half = model_width // 2
    hidden = w_gate.shape[1]
    vmem = pl.BlockSpec(memory_space=pltpu.VMEM)
    hbm = pl.BlockSpec(memory_space=pl.ANY)
    dma = pltpu.SemaphoreType.DMA
    spans = CHIPS * SLOTS
    return pl.pallas_call(
        kernel,
        out_shape=(
            jax.ShapeDtypeStruct(residual.shape, F32),
            jax.ShapeDtypeStruct((1, hidden, spans), F32),
        ),
        in_specs=[vmem] * 6 + [hbm] + [vmem] * 3 + [hbm] * 2,
        out_specs=(vmem, vmem),
        scratch_shapes=[
            pltpu.VMEM((SIDE, ST, HS), F32),
            pltpu.VMEM((SIDE, ST, HS), F32),
            pltpu.VMEM((ST, HS), F32),
            pltpu.VMEM((2 * HS, HS), F32),
            pltpu.VMEM((2, LC, HS), F32),
            pltpu.VMEM((2, LC, HS), F32),
            pltpu.VMEM((2 * LC, 2 * HS), BF),
            pltpu.VMEM((2 * HS, half), BF),
            pltpu.VMEM((2 * LC, half), BF),
            pltpu.VMEM((16, half), F32),
            pltpu.VMEM((2 * LC, half), BF),
            pltpu.VMEM((2,) + residual.shape, BF),
            pltpu.VMEM((16, half), F32),
            pltpu.VMEM((2, 16, half), F32),
            pltpu.VMEM((2 * LC, half), BF),
            pltpu.VMEM((4, CHIPS, LC), jnp.int32),
            pltpu.VMEM((4, CHIPS, LC), F32),
            pltpu.VMEM((2 * SLOTS, 2 * LC), BF),
            pltpu.VMEM((2, spans, half), BF),
            pltpu.VMEM((SLOTS, half), BF),
            pltpu.VMEM((8, spans), F32),
            pltpu.VMEM((hidden, model_width), BF),
            pltpu.VMEM((hidden, model_width), BF),
            dma((3,)),
            dma((SIDE,)),
            dma((SIDE,)),
            dma((SIDE,)),
            dma((SIDE,)),
            dma((5,)),
            dma((5,)),
            dma((CHIPS,)),
            dma((CHIPS,)),
            dma((CHIPS,)),
            dma((CHIPS,)),
            dma((2, SIDE * (SIDE + 1) + SIDE)),
            dma((2, CHIPS)),
        ],
        compiler_params=pltpu.CompilerParams(
            collective_id=0, has_side_effects=True, vmem_limit_bytes=48 << 20
        ),
        name="layer",
    )(
        queries,
        key_vecs,
        value_vecs,
        log_decay,
        head_gain.reshape(1, -1),
        residual,
        out_proj,
        norm_gain.reshape(1, -1),
        jnp.transpose(routes, (1, 2, 0)),
        jnp.transpose(route_weight, (1, 2, 0)),
        w_gate,
        w_up,
    )


def solution(mesh):
    placed = (
        P(("seq", "exp"), None, None),
        P(None, "seq", "exp"),
        P(None, "seq", "exp"),
        P(None, "seq", "exp"),
        P(None, "exp", "seq"),
        P("exp"),
        P("exp", None),
        P(),
        P(),
        P(),
        P("exp", "seq", None),
        P("exp", "seq", None),
    )
    return jax.shard_map(
        per_device,
        mesh=mesh,
        in_specs=placed,
        out_specs=(P(("seq", "exp"), None, None), P("exp", "seq", None)),
        check_vma=False,
    )
```

```python
import functools

import jax
import jax.numpy as jnp
from jax import lax
from jax.experimental import pallas as pl
from jax.experimental.pallas import tpu as pltpu
from jax.sharding import PartitionSpec as P

MESH = pl.DeviceIdType.MESH
BF = jnp.bfloat16
F32 = jnp.float32
SIDE = 4
CHIPS = 16
LC = 128
HS = 128
SLOTS = 32
PARTS = 3
EXTRA = 128
PARENT = {
    1: 0, 3: 0, 6: 0, 2: 3, 4: 3, 5: 6, 7: 6, 8: 6,
    -1: 0, -3: 0, -6: 0, -2: -3, -4: -3, -5: -6, -7: -6,
}
OFFS = list(PARENT)
CHILDREN = {p: [o for o in OFFS if PARENT[o] == p] for p in (0, 3, 6, -3, -6)}
LEAVES = [o for o in OFFS if o not in CHILDREN]
RELAYS = [o for o in OFFS if o in CHILDREN]
REACH = sorted({PARENT[o] - o for o in OFFS} | {o - PARENT[o] for o in OFFS})
ST = 2 * HS + 8


def dot(a, b, dims):
    return lax.dot_general(a, b, (dims, ((), ())), preferred_element_type=F32)


NN = ((1,), (0,))
NT = ((1,), (1,))
TN = ((0,), (0,))


def split(a):
    hi = a.astype(BF)
    return hi, (a - hi.astype(F32)).astype(BF)


def remote(src, dst, send, recv, peer):
    return pltpu.make_async_remote_copy(
        src, dst, send, recv, device_id=peer, device_id_type=MESH
    )


def kernel(
    q_hbm,
    k_hbm,
    v_hbm,
    ld_hbm,
    hg_hbm,
    res_hbm,
    outp_ref,
    ng_hbm,
    rt_hbm,
    wt_hbm,
    wg_ref,
    wu_ref,
    attn_ref,
    hid_ref,
    q_ref,
    k_ref,
    v_ref,
    ld_ref,
    hg_ref,
    ng_ref,
    rt_ref,
    wt_ref,
    ybuf,
    xbuf,
    prefix,
    inc,
    inner,
    grow,
    att,
    w2,
    part,
    full,
    rsbuf,
    rly,
    resbuf,
    res16,
    mix,
    nrm,
    rts,
    wts,
    picks,
    slots,
    other,
    sw,
    wgb,
    wub,
    gacc,
    uacc,
    lsem,
    ysend,
    yrecv,
    xsend,
    xrecv,
    bsend,
    brecv,
    zsend,
    zrecv,
    gsend,
    grecv,
    psend,
    precv,
    ssend,
    srecv,
):
    s = lax.axis_index("seq")
    e = lax.axis_index("exp")
    x, y, z, c = s // SIDE, s % SIDE, e // 2, e % 2
    half = mix.shape[2]
    depth = 2 * half

    drains = []

    def finish():
        for wait in drains:
            wait()

    def at(xx, yy, zz, cc):
        return (xx * SIDE + yy, zz * 2 + cc)

    sib = at(x, y, z, 1 - c)
    barrier = pltpu.get_barrier_semaphore()

    def greet(peer):
        pl.semaphore_signal(barrier, inc=1, device_id=peer, device_id_type=MESH)

    greet(sib)
    for d in range(1, SIDE):
        greet(at(x, (y + d) % SIDE, z, c))
        greet(at((x + d) % SIDE, y, z, c))

    for d in REACH:
        greet(at(x, y, (z + d) % CHIPS, c))

    mine = pl.ds(pl.multiple_of(c * half, half), half)
    theirs = pl.ds(pl.multiple_of((1 - c) * half, half), half)
    own_k = pl.ds(pl.multiple_of(c * HS, HS), HS)
    w2_own = pltpu.make_async_copy(outp_ref.at[:, mine], w2.at[own_k, :], lsem.at[0])
    wg_copy = pltpu.make_async_copy(wg_ref.at[0], wgb, lsem.at[1])
    wu_copy = pltpu.make_async_copy(wu_ref.at[0], wub, lsem.at[2])
    ins = [
        pltpu.make_async_copy(a, b, lsem.at[3 + i])
        for i, (a, b) in enumerate(
            (
                (ld_hbm, ld_ref),
                (k_hbm, k_ref),
                (v_hbm, v_ref),
                (q_hbm, q_ref),
                (rt_hbm, rt_ref),
                (wt_hbm, wt_ref),
                (hg_hbm, hg_ref),
                (ng_hbm, ng_ref),
                (res_hbm, resbuf.at[c]),
            )
        )
    ]
    for cp in ins:
        cp.start()
    w2_own.start()
    wg_copy.start()
    wu_copy.start()
    for cp in ins[:3]:
        cp.wait()

    ti = lax.broadcasted_iota(jnp.int32, (LC, LC), 0)
    ji = lax.broadcasted_iota(jnp.int32, (LC, LC), 1)
    causal = ji <= ti
    run_cols, run_rows = [], []
    for b in range(2):
        lb = jnp.broadcast_to(ld_ref[b], (LC, LC))
        rc = jnp.sum(jnp.where(causal, lb, 0.0), axis=1, keepdims=True)
        rr = jnp.sum(jnp.where(ji == ti, rc, 0.0), axis=0, keepdims=True)
        run_cols.append(rc)
        run_rows.append(rr)
        total = rr[:, LC - 1 :]
        kw = k_ref[b].astype(F32) * jnp.exp(total - rc)
        hi, lo = split(kw)
        vb = v_ref[b]
        ybuf[y, pl.ds(b * HS, HS), :] = dot(hi, vb, TN) + dot(lo, vb, TN)
        ybuf[y, pl.ds(2 * HS + b, 1), :] = jnp.broadcast_to(total, (1, HS))
    ybuf[y, pl.ds(2 * HS + 2, 6), :] = jnp.zeros((6, HS), F32)

    pl.semaphore_wait(barrier, 2 * (SIDE - 1) + 1 + len(REACH))

    for d in range(1, SIDE):
        cp = remote(
            ybuf.at[y], ybuf.at[y], ysend.at[d], yrecv.at[y], at(x, (y + d) % SIDE, z, c)
        )
        cp.start()
        drains.append(cp.wait_send)
    w2_sib = remote(outp_ref.at[:, theirs], w2.at[own_k, :], bsend.at[0], brecv.at[0], sib)
    w2_sib.start()
    drains.append(w2_sib.wait_send)
    res_sib = remote(res_hbm, resbuf.at[c], bsend.at[1], brecv.at[1], sib)
    res_sib.start()
    drains.append(res_sib.wait_send)
    for cp in ins[3:]:
        cp.wait()

    for b in range(2):
        rc, rr = run_cols[b], run_rows[b]
        decay = jnp.where(causal, jnp.exp(jnp.where(causal, rc - rr, 0.0)), 0.0)
        hi, lo = split(dot(q_ref[b], k_ref[b], NT) * decay)
        vb = v_ref[b]
        inner[b] = dot(hi, vb, NN) + dot(lo, vb, NN)
        grow[b] = jnp.broadcast_to(jnp.exp(rc), (LC, HS))

    for d in range(1, SIDE):
        yy = (y + d) % SIDE
        remote(
            ybuf.at[yy], ybuf.at[yy], ysend.at[d], yrecv.at[yy], at(x, yy, z, c)
        ).wait_recv()
    for b in range(2):
        rows = pl.ds(b * HS, HS)
        run = jnp.zeros((HS, HS), F32)
        logs = jnp.zeros((1, HS), F32)
        pre = jnp.zeros((HS, HS), F32)
        prelog = jnp.zeros((1, HS), F32)
        for i in range(SIDE):
            pre = jnp.where(y == i, run, pre)
            prelog = jnp.where(y == i, logs, prelog)
            tot = ybuf[i, pl.ds(2 * HS + b, 1), :]
            run = jnp.exp(tot) * run + ybuf[i, rows, :]
            logs = logs + tot
        prefix[rows, :] = pre
        prefix[pl.ds(2 * HS + b, 1), :] = prelog
        xbuf[x, rows, :] = run
        xbuf[x, pl.ds(2 * HS + b, 1), :] = logs
    xbuf[x, pl.ds(2 * HS + 2, 6), :] = jnp.zeros((6, HS), F32)
    for d in range(1, SIDE):

        @pl.when(x + d < SIDE)
        def _():
            remote(
                xbuf.at[x], xbuf.at[x], xsend.at[d], xrecv.at[x], at((x + d) % SIDE, y, z, c)
            ).start()

    def drain_x():
        for d in range(1, SIDE):

            @pl.when(x + d < SIDE)
            def _():
                remote(
                    xbuf.at[x], xbuf.at[x], xsend.at[d], xrecv.at[x], at((x + d) % SIDE, y, z, c)
                ).wait_send()

    drains.append(drain_x)

    for b in range(2):
        for kk in range(2):
            for blk in range(CHIPS):
                cols = pl.ds(blk * LC, LC)
                rts[b * 2 + kk, pl.ds(blk, 1), :] = rt_ref[b, pl.ds(kk, 1), cols]
                wts[b * 2 + kk, pl.ds(blk, 1), :] = wt_ref[b, pl.ds(kk, 1), cols]
    before = (ti < ji).astype(F32).astype(BF)
    slot_id = lax.broadcasted_iota(jnp.int32, (SLOTS, LC), 0).astype(F32)
    ri = lax.broadcasted_iota(jnp.int32, (2 * LC, 2 * LC), 0)
    ci = lax.broadcasted_iota(jnp.int32, (2 * LC, 2 * LC), 1)
    rb, rtm = ri // LC, ri % LC
    perm = (ci == (rtm // 8) * 16 + rb * 8 + rtm % 8).astype(F32).astype(BF)

    def places(h0, h1):
        first = dot((h0 + h1).astype(BF), before, NN)
        return first, first + h0

    for ex in range(2):
        hits = []
        for b in range(2):
            r0 = rts[b * 2, pl.ds(s, 1), :]
            r1 = rts[b * 2 + 1, pl.ds(s, 1), :]
            hit = ((r0 == z * 2 + ex) | (r1 == z * 2 + ex)).astype(F32)
            hits.append(jnp.broadcast_to(hit, (8, LC)))
        p0, p1 = places(hits[0], hits[1])
        table = []
        for hh, pp in ((hits[0], p0), (hits[1], p1)):
            one = jnp.where(slot_id == pp[0:1, :], hh[0:1, :], 0.0)
            table.append(one)
        table = jnp.concatenate(table, axis=1).astype(BF)
        picks[pl.ds(ex * SLOTS, SLOTS), :] = dot(table, perm, NN).astype(BF)

    hits = [((rts[b * 2] == e) | (rts[b * 2 + 1] == e)).astype(F32) for b in range(2)]
    tws = [
        jnp.where(rts[b * 2] == e, wts[b * 2], 0.0)
        + jnp.where(rts[b * 2 + 1] == e, wts[b * 2 + 1], 0.0)
        for b in range(2)
    ]
    ranks = places(hits[0], hits[1])
    for blk in range(CHIPS):
        acc = jnp.zeros((8, SLOTS), F32)
        for b in range(2):
            row = slice(blk, blk + 1)
            one = jnp.where(slot_id == ranks[b][row], hits[b][row], 0.0).astype(BF)
            w = jnp.broadcast_to(tws[b][row], (8, LC))
            hi = w.astype(BF)
            rest = w - hi.astype(F32)
            mid, low = split(rest)
            acc = acc + (dot(hi, one, NT) + (dot(mid, one, NT) + dot(low, one, NT)))
        sw[:, pl.ds(blk * SLOTS, SLOTS)] = acc

    inc[...] = jnp.zeros_like(inc)
    for i in range(SIDE - 1):

        @pl.when(x > i)
        def _():
            remote(
                xbuf.at[i], xbuf.at[i], xsend.at[0], xrecv.at[i], at(i, y, z, c)
            ).wait_recv()
            for b in range(2):
                rows = pl.ds(b * HS, HS)
                tot = xbuf[i, pl.ds(2 * HS + b, 1), :]
                inc[rows, :] = jnp.exp(tot) * inc[rows, :] + xbuf[i, rows, :]

    heads = []
    for b in range(2):
        rows = pl.ds(b * HS, HS)
        state = prefix[rows, :] + jnp.exp(prefix[pl.ds(2 * HS + b, 1), :]) * inc[rows, :]
        hi, lo = split(state)
        qb = q_ref[b]
        raw = inner[b] + grow[b] * (dot(qb, hi, NN) + dot(qb, lo, NN))
        meansq = jnp.mean(raw * raw, axis=1, keepdims=True)
        heads.append((raw * lax.rsqrt(meansq + 1e-06) * hg_ref[...]).reshape(CHIPS, 1, 8, HS))
    att[:, own_k] = jnp.concatenate(heads, axis=1).reshape(2 * LC, HS).astype(BF)
    att_sib = remote(att.at[:, own_k], att.at[:, own_k], bsend.at[2], brecv.at[2], sib)
    att_sib.start()
    drains.append(att_sib.wait_send)

    w2_own.wait()
    other_k = pl.ds(pl.multiple_of((1 - c) * HS, HS), HS)
    remote(outp_ref.at[:, theirs], w2.at[other_k, :], bsend.at[0], brecv.at[0], sib).wait_recv()
    remote(att.at[:, own_k], att.at[:, other_k], bsend.at[2], brecv.at[2], sib).wait_recv()
    width = half // PARTS

    def rows_of(zz):
        return pl.ds(pl.multiple_of((zz % CHIPS) * 16, 16), 16)

    def span(p):
        return pl.ds(p * width, width + (EXTRA if p == PARTS - 1 else 0))

    def send(cp):
        cp.start()
        drains.append(cp.wait_send)

    own_rows = rows_of(z)

    def rs_copy(o, p, src):
        i = OFFS.index(o)
        peer = at(x, y, (z - o + PARENT[o]) % CHIPS, c)
        dst = rsbuf.at[i, :, pl.ds(p * width, width)]
        return remote(src, dst, zsend.at[i, p], zrecv.at[i, p], peer)

    def rs_arrived(o, p):
        cols = pl.ds(p * width, width)
        i = OFFS.index(o)
        ref = rsbuf.at[i, :, cols]
        remote(ref, ref, zsend.at[i, p], zrecv.at[i, p], sib).wait_recv()
        return rsbuf[i, :, cols].astype(F32)

    def project(p):
        cols = pl.ds(p * width, width)
        got = dot(att[...], w2[:, cols], NN)
        full[:, cols] = got
        part[:, cols] = got.astype(BF)
        for o in LEAVES:
            send(rs_copy(o, p, part.at[rows_of(z - o), cols]))

    def relay(p):
        cols = pl.ds(p * width, width)
        for o in RELAYS:
            acc = full[rows_of(z - o), cols]
            for ch in CHILDREN[o]:
                acc = acc + rs_arrived(ch, p)
            r = RELAYS.index(o)
            rly[r, :, cols] = acc.astype(BF)
            send(rs_copy(o, p, rly.at[r, :, cols]))

    def ag_copy(o, p, src_z, peer):
        i = OFFS.index(o)
        ref = nrm.at[rows_of(src_z), span(p)]
        return remote(ref, ref, gsend.at[i, p], grecv.at[i, p], peer)

    def total(p):
        cols = pl.ds(p * width, width)
        acc = full[own_rows, cols] + res16[:, cols]
        for ch in CHILDREN[0]:
            acc = acc + rs_arrived(ch, p)
        mix[c, :, cols] = acc
        gain = ng_ref[:, pl.ds(pl.multiple_of(c * half + p * width, 128), width)]
        nrm[own_rows, cols] = (acc * gain).astype(BF)
        if p == PARTS - 1:
            mix_sib = remote(mix.at[c], mix.at[c], bsend.at[3], brecv.at[3], sib)
            send(mix_sib)
            near = mix[c]
            ss = jnp.sum(near * near, axis=1, keepdims=True)
            remote(mix.at[c], mix.at[1 - c], bsend.at[3], brecv.at[3], sib).wait_recv()
            far = mix[1 - c]
            ss = ss + jnp.sum(far * far, axis=1, keepdims=True)
            scale = lax.rsqrt(ss * (1.0 / depth) + 1e-06)
            hi = scale.astype(BF).astype(F32)
            mid = (scale - hi).astype(BF).astype(F32)
            low = scale - hi - mid
            lane = lax.broadcasted_iota(jnp.int32, (16, EXTRA), 1)
            extra = jnp.where(
                lane == 0, hi, jnp.where(lane == 1, mid, jnp.where(lane == 2, low, 0.0))
            )
            nrm[own_rows, pl.ds(half, EXTRA)] = extra.astype(BF)
        for o in CHILDREN[0]:
            send(ag_copy(o, p, z, at(x, y, (z + o) % CHIPS, c)))

    def forward(p):
        for o in RELAYS:
            ag_copy(o, p, z - o, sib).wait_recv()
            for ch in CHILDREN[o]:
                send(ag_copy(ch, p, z - o, at(x, y, (z - o + ch) % CHIPS, c)))

    theirs_p = pl.ds(pl.multiple_of((1 - c) * SLOTS, SLOTS), SLOTS)
    mine_p = pl.ds(pl.multiple_of(c * SLOTS, SLOTS), SLOTS)

    def pick(p):
        for o in LEAVES:
            ag_copy(o, p, z - o, sib).wait_recv()
        cols = span(p)
        other[:, cols] = dot(picks[theirs_p, :], nrm[:, cols], NN).astype(BF)
        send(
            remote(
                other.at[:, cols], slots.at[c, x, y, :, cols], psend.at[p], precv.at[p], sib
            )
        )
        slots[c, x, y, :, cols] = dot(picks[mine_p, :], nrm[:, cols], NN).astype(BF)

    def parts_of(p):
        size = width + (EXTRA if p == PARTS - 1 else 0)
        left = size // 256 * 128
        return pl.ds(p * width, left), pl.ds(p * width + left, size - left)

    def step1(h, d):
        dx, dy = (d, 0) if h == 0 else (0, d)
        return (x + dx) % SIDE, (y + dy) % SIDE

    def step2(h, d):
        dx, dy = (0, d) if h == 0 else (d, 0)
        return (x + dx) % SIDE, (y + dy) % SIDE

    def one(h, where, cols):
        return slots.at[h, where[0], where[1], :, cols]

    def four(h, where, cols):
        if h == 0:
            return slots.at[h, :, where[1], :, cols]
        return slots.at[h, where[0], :, :, cols]

    def xy(h, p, stage, i, ref, where):
        return remote(
            ref, ref, ssend.at[h, p, stage, i], srecv.at[h, p, stage, i], at(*where, z, c)
        )

    def hop1(p):
        cols = span(p)
        remote(
            other.at[:, cols], slots.at[1 - c, x, y, :, cols], psend.at[p], precv.at[p], sib
        ).wait_recv()
        for h in range(2):
            for i, d in enumerate((1, -1)):
                send(xy(h, p, 0, i, one(h, (x, y), cols), step1(h, d)))

    def hop2(p):
        for h in range(2):
            for i, d in enumerate((1, -1)):
                back = step1(h, -d)
                xy(h, p, 0, i, one(h, back, span(p)), back).wait_recv()
                send(xy(h, p, 1, i, one(h, back, parts_of(p)[i]), step1(h, d)))

    def hop3(p):
        for h in range(2):
            for i, d in enumerate((1, -1)):
                far = step1(h, 2)
                xy(h, p, 1, i, one(h, far, parts_of(p)[i]), far).wait_recv()
            for i, d in enumerate((1, -1)):
                send(xy(h, p, 2, i, four(h, (x, y), span(p)), step2(h, d)))

    def hop4(p):
        for h in range(2):
            for i, d in enumerate((1, -1)):
                back = step2(h, -d)
                xy(h, p, 2, i, four(h, back, span(p)), back).wait_recv()
                send(xy(h, p, 3, i, four(h, back, parts_of(p)[i]), step2(h, d)))

    def multiply(p):
        for h in range(2):
            for i in range(2):
                far = step2(h, 2)
                xy(h, p, 3, i, four(h, far, parts_of(p)[i]), far).wait_recv()
        if p == 0:
            wg_copy.wait()
            wu_copy.wait()
        for n in range(2):
            rows = pl.ds(n * 256, 256)
            for w, acc in ((wgb, gacc), (wub, uacc)):
                got = None
                for h in range(2):
                    rhs = slots[h, pl.ds(2 * n, 2), :, :, pl.ds(p * width, width)]
                    rhs = rhs.reshape(256, width)
                    term = dot(w[:, pl.ds(h * half + p * width, width)], rhs, NT)
                    got = term if got is None else got + term
                acc[:, rows] = got if p == 0 else acc[:, rows] + got

    remote(res_hbm, resbuf.at[1 - c], bsend.at[1], brecv.at[1], sib).wait_recv()
    for cc in range(2):
        for i in range(4):
            two = resbuf[cc, i, :, mine].astype(F32)
            for b in range(2):
                res16[pl.ds(b * 8 + cc * 4 + i, 1), :] = two[b : b + 1, :]
    for p in range(PARTS):
        project(p)
    stages = [relay, total, forward, pick, hop1, hop2, hop3, hop4, multiply]
    for t in range(len(stages) + PARTS - 1):
        for p in range(PARTS):
            if 0 <= t - p < len(stages):
                stages[t - p](p)

    for h in range(2):
        for b in range(2):
            for i in range(4):
                attn_ref[i, pl.ds(b, 1), pl.ds(h * half, half)] = mix[
                    h, pl.ds(b * 8 + c * 4 + i, 1), :
                ]
    lane = lax.broadcasted_iota(jnp.int32, (8, EXTRA), 1)
    ones = jnp.where(lane < 3, 1.0, 0.0).astype(BF)
    for n in range(2):
        rows = pl.ds(n * 256, 256)
        extra = slots[0, pl.ds(2 * n, 2), :, :, pl.ds(half, EXTRA)].reshape(256, EXTRA)
        scale = dot(ones, extra, NT)[0:1, :]
        gate = gacc[:, rows] * scale
        hid_ref[0, :, rows] = (sw[0:1, rows] * scale) * (
            gate / (1.0 + jnp.exp(-gate)) * uacc[:, rows]
        )
    finish()


def per_device(
    residual,
    queries,
    key_vecs,
    value_vecs,
    log_decay,
    head_gain,
    out_proj,
    norm_gain,
    routes,
    route_weight,
    w_gate,
    w_up,
):
    model_width = residual.shape[2]
    half = model_width // 2
    hidden = w_gate.shape[1]
    vmem = pl.BlockSpec(memory_space=pltpu.VMEM)
    hbm = pl.BlockSpec(memory_space=pltpu.HBM)
    dma = pltpu.SemaphoreType.DMA
    spans = CHIPS * SLOTS
    return pl.pallas_call(
        kernel,
        out_shape=(
            jax.ShapeDtypeStruct(residual.shape, F32),
            jax.ShapeDtypeStruct((1, hidden, spans), F32),
        ),
        in_specs=[hbm] * 12,
        out_specs=(vmem, vmem),
        scratch_shapes=[
            pltpu.VMEM(queries.shape, BF),
            pltpu.VMEM(queries.shape, BF),
            pltpu.VMEM(queries.shape, BF),
            pltpu.VMEM(log_decay.shape, F32),
            pltpu.VMEM((1, HS), F32),
            pltpu.VMEM((1, model_width), F32),
            pltpu.VMEM((2, 2, CHIPS * LC), jnp.int32),
            pltpu.VMEM((2, 2, CHIPS * LC), F32),
            pltpu.VMEM((SIDE, ST, HS), F32),
            pltpu.VMEM((SIDE, ST, HS), F32),
            pltpu.VMEM((ST, HS), F32),
            pltpu.VMEM((2 * HS, HS), F32),
            pltpu.VMEM((2, LC, HS), F32),
            pltpu.VMEM((2, LC, HS), F32),
            pltpu.VMEM((2 * LC, 2 * HS), BF),
            pltpu.VMEM((2 * HS, half), BF),
            pltpu.VMEM((2 * LC, half), BF),
            pltpu.VMEM((2 * LC, half), F32),
            pltpu.VMEM((len(OFFS), 16, half), BF),
            pltpu.VMEM((len(RELAYS), 16, half), BF),
            pltpu.VMEM((2,) + residual.shape, BF),
            pltpu.VMEM((16, half), F32),
            pltpu.VMEM((2, 16, half), F32),
            pltpu.VMEM((2 * LC, half + EXTRA), BF),
            pltpu.VMEM((4, CHIPS, LC), jnp.int32),
            pltpu.VMEM((4, CHIPS, LC), F32),
            pltpu.VMEM((2 * SLOTS, 2 * LC), BF),
            pltpu.VMEM((2, SIDE, SIDE, SLOTS, half + EXTRA), BF),
            pltpu.VMEM((SLOTS, half + EXTRA), BF),
            pltpu.VMEM((8, spans), F32),
            pltpu.VMEM((hidden, model_width), BF),
            pltpu.VMEM((hidden, model_width), BF),
            pltpu.VMEM((hidden, spans), F32),
            pltpu.VMEM((hidden, spans), F32),
            dma((12,)),
            dma((SIDE,)),
            dma((SIDE,)),
            dma((SIDE,)),
            dma((SIDE,)),
            dma((5,)),
            dma((5,)),
            dma((len(OFFS), PARTS)),
            dma((len(OFFS), PARTS)),
            dma((len(OFFS), PARTS)),
            dma((len(OFFS), PARTS)),
            dma((PARTS,)),
            dma((PARTS,)),
            dma((2, PARTS, 4, 2)),
            dma((2, PARTS, 4, 2)),
        ],
        compiler_params=pltpu.CompilerParams(
            collective_id=0, has_side_effects=True, vmem_limit_bytes=48 << 20
        ),
        name="layer",
    )(*[pltpu.with_memory_space_constraint(a, pltpu.HBM) for a in (
        queries,
        key_vecs,
        value_vecs,
        log_decay,
        head_gain.reshape(1, -1),
        residual,
        out_proj,
        norm_gain.reshape(1, -1),
        jnp.transpose(routes, (1, 2, 0)),
        jnp.transpose(route_weight, (1, 2, 0)),
        w_gate,
        w_up,
    )])


def solution(mesh):
    placed = (
        P(("seq", "exp"), None, None),
        P(None, "seq", "exp"),
        P(None, "seq", "exp"),
        P(None, "seq", "exp"),
        P(None, "exp", "seq"),
        P("exp"),
        P("exp", None),
        P(),
        P(),
        P(),
        P("exp", "seq", None),
        P("exp", "seq", None),
    )
    return jax.shard_map(
        per_device,
        mesh=mesh,
        in_specs=placed,
        out_specs=(P(("seq", "exp"), None, None), P("exp", "seq", None)),
        check_vma=False,
    )
```

```python
import functools

import jax
import jax.numpy as jnp
from jax import lax
from jax.experimental import pallas as pl
from jax.experimental.pallas import tpu as pltpu
from jax.sharding import PartitionSpec as P

MESH = pl.DeviceIdType.MESH
BF = jnp.bfloat16
F32 = jnp.float32
SIDE = 4
CHIPS = 16
BLOCKS = SIDE * SIDE
SHARE = 16
LC = 128
HS = 128
SLOTS = 32
PARTS = 3
EXTRA = 128
PARENT = {
    1: 0, 3: 0, 6: 3, 2: 3, 4: 3, 5: 6, 7: 6, 8: 6,
    -1: 0, -3: 0, -6: -3, -2: -3, -4: -3, -5: -6, -7: -6,
}
OFFS = list(PARENT)
CHILDREN = {p: [o for o in OFFS if PARENT[o] == p] for p in set(PARENT.values())}
LEAVES = [o for o in OFFS if o not in CHILDREN]
RELAYS = [o for o in OFFS if o in CHILDREN]


def depth_of(o):
    return 0 if o == 0 else 1 + depth_of(PARENT[o])


DEPTH = max(depth_of(o) for o in RELAYS)
REACH = sorted({PARENT[o] - o for o in OFFS} | {o - PARENT[o] for o in OFFS})


def dot(a, b, dims):
    return lax.dot_general(a, b, (dims, ((), ())), preferred_element_type=F32)


NN = ((1,), (0,))
NT = ((1,), (1,))
TN = ((0,), (0,))


def split(a):
    hi = a.astype(BF)
    return hi, (a - hi.astype(F32)).astype(BF)


def remote(src, dst, send, recv, peer):
    return pltpu.make_async_remote_copy(
        src, dst, send, recv, device_id=peer, device_id_type=MESH
    )


def kernel(
    q_hbm,
    k_hbm,
    v_hbm,
    ld_hbm,
    hg_hbm,
    res_hbm,
    outp_ref,
    ng_hbm,
    rt_hbm,
    wt_hbm,
    wg_ref,
    wu_ref,
    attn_ref,
    hid_ref,
    q_ref,
    k_ref,
    v_ref,
    ld_ref,
    hg_ref,
    ng_ref,
    rt_ref,
    wt_ref,
    out1,
    in1,
    out2,
    inc,
    inner,
    grow,
    att,
    w2,
    part,
    full,
    rsbuf,
    rly,
    resbuf,
    res16,
    mix,
    nrm,
    rts,
    wts,
    picks,
    slots,
    other,
    sw,
    wgb,
    wub,
    gacc,
    uacc,
    lsem,
    asend,
    arecv,
    xsend,
    xrecv,
    bsend,
    brecv,
    zsend,
    zrecv,
    gsend,
    grecv,
    psend,
    precv,
    ssend,
    srecv,
):
    s = lax.axis_index("seq")
    e = lax.axis_index("exp")
    x, y, z, c = s // SIDE, s % SIDE, e // 2, e % 2
    half = mix.shape[2]
    depth = 2 * half

    drains = []

    def finish():
        for wait in drains:
            wait()

    def at(xx, yy, zz, cc):
        return (xx * SIDE + yy, zz * 2 + cc)

    sib = at(x, y, z, 1 - c)
    barrier = pltpu.get_barrier_semaphore()

    def greet(peer):
        pl.semaphore_signal(barrier, inc=1, device_id=peer, device_id_type=MESH)

    mine = pl.ds(pl.multiple_of(c * half, half), half)
    theirs = pl.ds(pl.multiple_of((1 - c) * half, half), half)
    own_k = pl.ds(pl.multiple_of(c * HS, HS), HS)
    w2_own = pltpu.make_async_copy(outp_ref.at[:, mine], w2.at[own_k, :], lsem.at[0])
    wg_copy = pltpu.make_async_copy(wg_ref.at[0], wgb, lsem.at[1])
    wu_copy = pltpu.make_async_copy(wu_ref.at[0], wub, lsem.at[2])
    ins = [
        pltpu.make_async_copy(a, b, lsem.at[3 + i])
        for i, (a, b) in enumerate(
            (
                (ld_hbm, ld_ref),
                (k_hbm, k_ref),
                (v_hbm, v_ref),
                (q_hbm, q_ref),
                (rt_hbm, rt_ref),
                (wt_hbm, wt_ref),
                (hg_hbm, hg_ref),
                (ng_hbm, ng_ref),
                (res_hbm, resbuf.at[c]),
            )
        )
    ]
    for cp in ins:
        cp.start()
    w2_own.start()
    wg_copy.start()
    wu_copy.start()
    greet(sib)

    def greet_xy(d, _):
        greet(((s + d) % BLOCKS, e))
        return 0

    lax.fori_loop(1, BLOCKS, greet_xy, 0)
    for d in REACH:
        greet(at(x, y, (z + d) % CHIPS, c))

    for cp in ins[:3]:
        cp.wait()

    ti = lax.broadcasted_iota(jnp.int32, (LC, LC), 0)
    ji = lax.broadcasted_iota(jnp.int32, (LC, LC), 1)
    causal = ji <= ti
    run_cols, run_rows = [], []
    for b in range(2):
        lb = jnp.broadcast_to(ld_ref[b], (LC, LC))
        rc = jnp.sum(jnp.where(causal, lb, 0.0), axis=1, keepdims=True)
        rr = jnp.sum(jnp.where(ji == ti, rc, 0.0), axis=0, keepdims=True)
        run_cols.append(rc)
        run_rows.append(rr)
        total = rr[:, LC - 1 :]
        kw = k_ref[b].astype(F32) * jnp.exp(total - rc)
        hi, lo = split(kw)
        vb = v_ref[b]
        fresh = dot(hi, vb, TN) + dot(lo, vb, TN)
        lines = jnp.broadcast_to(total, (8, HS))
        for i in range(HS // SHARE):
            j = b * (HS // SHARE) + i
            out1[j, pl.ds(0, SHARE), :] = fresh[i * SHARE : (i + 1) * SHARE]
            out1[j, pl.ds(SHARE, 8), :] = lines

    pl.semaphore_wait(barrier, BLOCKS + len(REACH))

    def order(i):
        return BLOCKS // 2 + ((i + 1) // 2) * (1 - 2 * (i % 2))

    def first(j):
        return remote(out1.at[j], in1.at[s], asend.at[j], arecv.at[s], (j, e))

    def second(j):
        return remote(out2.at[j], inc.at[s], xsend.at[j], xrecv.at[s], (j, e))

    def loop(body, start=1):
        def turn(i, _):
            body((s + (order(i) if start == 0 else i)) % BLOCKS)
            return 0

        lax.fori_loop(start, BLOCKS - 1 + start, turn, 0)

    loop(lambda j: first(j).start(), 0)
    drains.append(lambda: loop(lambda j: first(j).wait_send()))
    in1[s] = out1[s]
    w2_sib = remote(outp_ref.at[:, theirs], w2.at[own_k, :], bsend.at[0], brecv.at[0], sib)
    w2_sib.start()
    drains.append(w2_sib.wait_send)
    res_sib = remote(res_hbm, resbuf.at[c], bsend.at[1], brecv.at[1], sib)
    res_sib.start()
    drains.append(res_sib.wait_send)
    for cp in ins[3:]:
        cp.wait()

    for b in range(2):
        rc, rr = run_cols[b], run_rows[b]
        decay = jnp.where(causal, jnp.exp(jnp.where(causal, rc - rr, 0.0)), 0.0)
        hi, lo = split(dot(q_ref[b], k_ref[b], NT) * decay)
        vb = v_ref[b]
        inner[b] = dot(hi, vb, NN) + dot(lo, vb, NN)
        grow[b] = jnp.broadcast_to(jnp.exp(rc), (LC, HS))

    loop(lambda j: remote(in1.at[j], in1.at[j], asend.at[j], arecv.at[j], (j, e)).wait_recv())
    run = jnp.zeros((SHARE, HS), F32)
    for j in range(BLOCKS):
        out2[j] = run
        keep = jnp.exp(in1[j, pl.ds(SHARE, 8), :])
        run = jnp.concatenate([keep] * (SHARE // 8), axis=0) * run + in1[j, pl.ds(0, SHARE), :]
    loop(lambda j: second(j).start(), 0)
    drains.append(lambda: loop(lambda j: second(j).wait_send()))
    inc[s] = out2[s]

    for b in range(2):
        for kk in range(2):
            for blk in range(CHIPS):
                cols = pl.ds(blk * LC, LC)
                rts[b * 2 + kk, pl.ds(blk, 1), :] = rt_ref[b, pl.ds(kk, 1), cols]
                wts[b * 2 + kk, pl.ds(blk, 1), :] = wt_ref[b, pl.ds(kk, 1), cols]
    before = (ti < ji).astype(F32).astype(BF)
    slot_id = lax.broadcasted_iota(jnp.int32, (SLOTS, LC), 0).astype(F32)
    ri = lax.broadcasted_iota(jnp.int32, (2 * LC, 2 * LC), 0)
    ci = lax.broadcasted_iota(jnp.int32, (2 * LC, 2 * LC), 1)
    rb, rtm = ri // LC, ri % LC
    perm = (ci == (rtm // 8) * 16 + rb * 8 + rtm % 8).astype(F32).astype(BF)

    def places(h0, h1):
        first = dot((h0 + h1).astype(BF), before, NN)
        return first, first + h0

    for ex in range(2):
        hits = []
        for b in range(2):
            r0 = rts[b * 2, pl.ds(s, 1), :]
            r1 = rts[b * 2 + 1, pl.ds(s, 1), :]
            hit = ((r0 == z * 2 + ex) | (r1 == z * 2 + ex)).astype(F32)
            hits.append(jnp.broadcast_to(hit, (8, LC)))
        p0, p1 = places(hits[0], hits[1])
        table = []
        for hh, pp in ((hits[0], p0), (hits[1], p1)):
            one = jnp.where(slot_id == pp[0:1, :], hh[0:1, :], 0.0)
            table.append(one)
        table = jnp.concatenate(table, axis=1).astype(BF)
        picks[pl.ds(ex * SLOTS, SLOTS), :] = dot(table, perm, NN).astype(BF)

    hits = [((rts[b * 2] == e) | (rts[b * 2 + 1] == e)).astype(F32) for b in range(2)]
    tws = [
        jnp.where(rts[b * 2] == e, wts[b * 2], 0.0)
        + jnp.where(rts[b * 2 + 1] == e, wts[b * 2 + 1], 0.0)
        for b in range(2)
    ]
    ranks = places(hits[0], hits[1])
    for blk in range(CHIPS):
        acc = jnp.zeros((8, SLOTS), F32)
        for b in range(2):
            row = slice(blk, blk + 1)
            one = jnp.where(slot_id == ranks[b][row], hits[b][row], 0.0).astype(BF)
            w = jnp.broadcast_to(tws[b][row], (8, LC))
            hi = w.astype(BF)
            rest = w - hi.astype(F32)
            mid, low = split(rest)
            acc = acc + (dot(hi, one, NT) + (dot(mid, one, NT) + dot(low, one, NT)))
        sw[:, pl.ds(blk * SLOTS, SLOTS)] = acc

    loop(lambda j: remote(inc.at[j], inc.at[j], xsend.at[j], xrecv.at[j], (j, e)).wait_recv())
    heads = []
    for b in range(2):
        state = inc[pl.ds(b * (HS // SHARE), HS // SHARE)].reshape(HS, HS)
        hi, lo = split(state)
        qb = q_ref[b]
        raw = inner[b] + grow[b] * (dot(qb, hi, NN) + dot(qb, lo, NN))
        meansq = jnp.mean(raw * raw, axis=1, keepdims=True)
        heads.append((raw * lax.rsqrt(meansq + 1e-06) * hg_ref[...]).reshape(CHIPS, 1, 8, HS))
    att[:, own_k] = jnp.concatenate(heads, axis=1).reshape(2 * LC, HS).astype(BF)
    att_sib = remote(att.at[:, own_k], att.at[:, own_k], bsend.at[2], brecv.at[2], sib)
    att_sib.start()
    drains.append(att_sib.wait_send)

    w2_own.wait()
    other_k = pl.ds(pl.multiple_of((1 - c) * HS, HS), HS)
    remote(outp_ref.at[:, theirs], w2.at[other_k, :], bsend.at[0], brecv.at[0], sib).wait_recv()
    remote(att.at[:, own_k], att.at[:, other_k], bsend.at[2], brecv.at[2], sib).wait_recv()
    width = half // PARTS

    def rows_of(zz):
        return pl.ds(pl.multiple_of((zz % CHIPS) * 16, 16), 16)

    def span(p):
        return pl.ds(p * width, width + (EXTRA if p == PARTS - 1 else 0))

    def send(cp):
        cp.start()
        drains.append(cp.wait_send)

    own_rows = rows_of(z)

    def rs_copy(o, p, src):
        i = OFFS.index(o)
        peer = at(x, y, (z - o + PARENT[o]) % CHIPS, c)
        dst = rsbuf.at[i, :, pl.ds(p * width, width)]
        return remote(src, dst, zsend.at[i, p], zrecv.at[i, p], peer)

    def rs_arrived(o, p):
        cols = pl.ds(p * width, width)
        i = OFFS.index(o)
        ref = rsbuf.at[i, :, cols]
        remote(ref, ref, zsend.at[i, p], zrecv.at[i, p], sib).wait_recv()
        return rsbuf[i, :, cols].astype(F32)

    def project(p):
        cols = pl.ds(p * width, width)
        got = dot(att[...], w2[:, cols], NN)
        full[:, cols] = got
        part[:, cols] = got.astype(BF)
        for o in LEAVES:
            send(rs_copy(o, p, part.at[rows_of(z - o), cols]))

    def relay(level, p):
        cols = pl.ds(p * width, width)
        for o in RELAYS:
            if depth_of(o) != level:
                continue
            acc = full[rows_of(z - o), cols]
            for ch in CHILDREN[o]:
                acc = acc + rs_arrived(ch, p)
            r = RELAYS.index(o)
            rly[r, :, cols] = acc.astype(BF)
            send(rs_copy(o, p, rly.at[r, :, cols]))

    def ag_copy(o, p, src_z, peer):
        i = OFFS.index(o)
        ref = nrm.at[rows_of(src_z), span(p)]
        return remote(ref, ref, gsend.at[i, p], grecv.at[i, p], peer)

    def total(p):
        cols = pl.ds(p * width, width)
        acc = full[own_rows, cols] + res16[:, cols]
        for ch in CHILDREN[0]:
            acc = acc + rs_arrived(ch, p)
        mix[c, :, cols] = acc
        gain = ng_ref[:, pl.ds(pl.multiple_of(c * half + p * width, 128), width)]
        nrm[own_rows, cols] = (acc * gain).astype(BF)
        if p == PARTS - 1:
            mix_sib = remote(mix.at[c], mix.at[c], bsend.at[3], brecv.at[3], sib)
            send(mix_sib)
            near = mix[c]
            ss = jnp.sum(near * near, axis=1, keepdims=True)
            remote(mix.at[c], mix.at[1 - c], bsend.at[3], brecv.at[3], sib).wait_recv()
            far = mix[1 - c]
            ss = ss + jnp.sum(far * far, axis=1, keepdims=True)
            scale = lax.rsqrt(ss * (1.0 / depth) + 1e-06)
            hi = scale.astype(BF).astype(F32)
            mid = (scale - hi).astype(BF).astype(F32)
            low = scale - hi - mid
            lane = lax.broadcasted_iota(jnp.int32, (16, EXTRA), 1)
            extra = jnp.where(
                lane == 0, hi, jnp.where(lane == 1, mid, jnp.where(lane == 2, low, 0.0))
            )
            nrm[own_rows, pl.ds(half, EXTRA)] = extra.astype(BF)
        for o in CHILDREN[0]:
            send(ag_copy(o, p, z, at(x, y, (z + o) % CHIPS, c)))

    def forward(level, p):
        for o in RELAYS:
            if depth_of(o) != level:
                continue
            ag_copy(o, p, z - o, sib).wait_recv()
            for ch in CHILDREN[o]:
                send(ag_copy(ch, p, z - o, at(x, y, (z - o + ch) % CHIPS, c)))

    theirs_p = pl.ds(pl.multiple_of((1 - c) * SLOTS, SLOTS), SLOTS)
    mine_p = pl.ds(pl.multiple_of(c * SLOTS, SLOTS), SLOTS)

    def pick(p):
        for o in LEAVES:
            ag_copy(o, p, z - o, sib).wait_recv()
        cols = span(p)
        other[:, cols] = dot(picks[theirs_p, :], nrm[:, cols], NN).astype(BF)
        send(
            remote(
                other.at[:, cols], slots.at[c, x, y, :, cols], psend.at[p], precv.at[p], sib
            )
        )
        slots[c, x, y, :, cols] = dot(picks[mine_p, :], nrm[:, cols], NN).astype(BF)

    def parts_of(p):
        size = width + (EXTRA if p == PARTS - 1 else 0)
        left = size // 256 * 128
        return pl.ds(p * width, left), pl.ds(p * width + left, size - left)

    def step1(h, d):
        dx, dy = (d, 0) if h == 0 else (0, d)
        return (x + dx) % SIDE, (y + dy) % SIDE

    def step2(h, d):
        dx, dy = (0, d) if h == 0 else (d, 0)
        return (x + dx) % SIDE, (y + dy) % SIDE

    def one(h, where, cols):
        return slots.at[h, where[0], where[1], :, cols]

    def four(h, where, cols):
        if h == 0:
            return slots.at[h, :, where[1], :, cols]
        return slots.at[h, where[0], :, :, cols]

    def xy(h, p, stage, i, ref, where):
        return remote(
            ref, ref, ssend.at[h, p, stage, i], srecv.at[h, p, stage, i], at(*where, z, c)
        )

    def hop1(p):
        cols = span(p)
        remote(
            other.at[:, cols], slots.at[1 - c, x, y, :, cols], psend.at[p], precv.at[p], sib
        ).wait_recv()
        for h in range(2):
            for i, d in enumerate((1, -1)):
                send(xy(h, p, 0, i, one(h, (x, y), cols), step1(h, d)))

    def hop2(p):
        for h in range(2):
            for i, d in enumerate((1, -1)):
                back = step1(h, -d)
                xy(h, p, 0, i, one(h, back, span(p)), back).wait_recv()
                send(xy(h, p, 1, i, one(h, back, parts_of(p)[i]), step1(h, d)))

    def hop3(p):
        for h in range(2):
            for i, d in enumerate((1, -1)):
                far = step1(h, 2)
                xy(h, p, 1, i, one(h, far, parts_of(p)[i]), far).wait_recv()
            for i, d in enumerate((1, -1)):
                send(xy(h, p, 2, i, four(h, (x, y), span(p)), step2(h, d)))

    def hop4(p):
        for h in range(2):
            for i, d in enumerate((1, -1)):
                back = step2(h, -d)
                xy(h, p, 2, i, four(h, back, span(p)), back).wait_recv()
                send(xy(h, p, 3, i, four(h, back, parts_of(p)[i]), step2(h, d)))

    def multiply(p):
        for h in range(2):
            for i in range(2):
                far = step2(h, 2)
                xy(h, p, 3, i, four(h, far, parts_of(p)[i]), far).wait_recv()
        if p == 0:
            wg_copy.wait()
            wu_copy.wait()
        for n in range(2):
            rows = pl.ds(n * 256, 256)
            for w, acc in ((wgb, gacc), (wub, uacc)):
                got = None
                for h in range(2):
                    rhs = slots[h, pl.ds(2 * n, 2), :, :, pl.ds(p * width, width)]
                    rhs = rhs.reshape(256, width)
                    term = dot(w[:, pl.ds(h * half + p * width, width)], rhs, NT)
                    got = term if got is None else got + term
                acc[:, rows] = got if p == 0 else acc[:, rows] + got

    remote(res_hbm, resbuf.at[1 - c], bsend.at[1], brecv.at[1], sib).wait_recv()
    for cc in range(2):
        for i in range(4):
            two = resbuf[cc, i, :, mine].astype(F32)
            for b in range(2):
                res16[pl.ds(b * 8 + cc * 4 + i, 1), :] = two[b : b + 1, :]
    for p in range(PARTS):
        project(p)
    stages = [functools.partial(relay, n) for n in range(DEPTH, 0, -1)] + [total]
    stages += [functools.partial(forward, n) for n in range(1, DEPTH + 1)]
    stages += [pick, hop1, hop2, hop3, hop4, multiply]
    for stage in stages:
        for p in range(PARTS):
            stage(p)

    for h in range(2):
        for b in range(2):
            for i in range(4):
                attn_ref[i, pl.ds(b, 1), pl.ds(h * half, half)] = mix[
                    h, pl.ds(b * 8 + c * 4 + i, 1), :
                ]
    lane = lax.broadcasted_iota(jnp.int32, (8, EXTRA), 1)
    ones = jnp.where(lane < 3, 1.0, 0.0).astype(BF)
    for n in range(2):
        rows = pl.ds(n * 256, 256)
        extra = slots[0, pl.ds(2 * n, 2), :, :, pl.ds(half, EXTRA)].reshape(256, EXTRA)
        scale = dot(ones, extra, NT)[0:1, :]
        gate = gacc[:, rows] * scale
        hid_ref[0, :, rows] = (sw[0:1, rows] * scale) * (
            gate / (1.0 + jnp.exp(-gate)) * uacc[:, rows]
        )
    finish()


def per_device(
    residual,
    queries,
    key_vecs,
    value_vecs,
    log_decay,
    head_gain,
    out_proj,
    norm_gain,
    routes,
    route_weight,
    w_gate,
    w_up,
):
    model_width = residual.shape[2]
    half = model_width // 2
    hidden = w_gate.shape[1]
    vmem = pl.BlockSpec(memory_space=pltpu.VMEM)
    hbm = pl.BlockSpec(memory_space=pltpu.HBM)
    dma = pltpu.SemaphoreType.DMA
    spans = CHIPS * SLOTS
    return pl.pallas_call(
        kernel,
        out_shape=(
            jax.ShapeDtypeStruct(residual.shape, F32),
            jax.ShapeDtypeStruct((1, hidden, spans), F32),
        ),
        in_specs=[hbm] * 12,
        out_specs=(vmem, vmem),
        scratch_shapes=[
            pltpu.VMEM(queries.shape, BF),
            pltpu.VMEM(queries.shape, BF),
            pltpu.VMEM(queries.shape, BF),
            pltpu.VMEM(log_decay.shape, F32),
            pltpu.VMEM((1, HS), F32),
            pltpu.VMEM((1, model_width), F32),
            pltpu.VMEM((2, 2, CHIPS * LC), jnp.int32),
            pltpu.VMEM((2, 2, CHIPS * LC), F32),
            pltpu.VMEM((BLOCKS, SHARE + 8, HS), F32),
            pltpu.VMEM((BLOCKS, SHARE + 8, HS), F32),
            pltpu.VMEM((BLOCKS, SHARE, HS), F32),
            pltpu.VMEM((BLOCKS, SHARE, HS), F32),
            pltpu.VMEM((2, LC, HS), F32),
            pltpu.VMEM((2, LC, HS), F32),
            pltpu.VMEM((2 * LC, 2 * HS), BF),
            pltpu.VMEM((2 * HS, half), BF),
            pltpu.VMEM((2 * LC, half), BF),
            pltpu.VMEM((2 * LC, half), F32),
            pltpu.VMEM((len(OFFS), 16, half), BF),
            pltpu.VMEM((len(RELAYS), 16, half), BF),
            pltpu.VMEM((2,) + residual.shape, BF),
            pltpu.VMEM((16, half), F32),
            pltpu.VMEM((2, 16, half), F32),
            pltpu.VMEM((2 * LC, half + EXTRA), BF),
            pltpu.VMEM((4, CHIPS, LC), jnp.int32),
            pltpu.VMEM((4, CHIPS, LC), F32),
            pltpu.VMEM((2 * SLOTS, 2 * LC), BF),
            pltpu.VMEM((2, SIDE, SIDE, SLOTS, half + EXTRA), BF),
            pltpu.VMEM((SLOTS, half + EXTRA), BF),
            pltpu.VMEM((8, spans), F32),
            pltpu.VMEM((hidden, model_width), BF),
            pltpu.VMEM((hidden, model_width), BF),
            pltpu.VMEM((hidden, spans), F32),
            pltpu.VMEM((hidden, spans), F32),
            dma((12,)),
            dma((BLOCKS,)),
            dma((BLOCKS,)),
            dma((BLOCKS,)),
            dma((BLOCKS,)),
            dma((5,)),
            dma((5,)),
            dma((len(OFFS), PARTS)),
            dma((len(OFFS), PARTS)),
            dma((len(OFFS), PARTS)),
            dma((len(OFFS), PARTS)),
            dma((PARTS,)),
            dma((PARTS,)),
            dma((2, PARTS, 4, 2)),
            dma((2, PARTS, 4, 2)),
        ],
        compiler_params=pltpu.CompilerParams(
            collective_id=0, has_side_effects=True, vmem_limit_bytes=48 << 20
        ),
        name="layer",
    )(*[pltpu.with_memory_space_constraint(a, pltpu.HBM) for a in (
        queries,
        key_vecs,
        value_vecs,
        log_decay,
        head_gain.reshape(1, -1),
        residual,
        out_proj,
        norm_gain.reshape(1, -1),
        jnp.transpose(routes, (1, 2, 0)),
        jnp.transpose(route_weight, (1, 2, 0)),
        w_gate,
        w_up,
    )])


def solution(mesh):
    placed = (
        P(("seq", "exp"), None, None),
        P(None, "seq", "exp"),
        P(None, "seq", "exp"),
        P(None, "seq", "exp"),
        P(None, "exp", "seq"),
        P("exp"),
        P("exp", None),
        P(),
        P(),
        P(),
        P("exp", "seq", None),
        P("exp", "seq", None),
    )
    return jax.shard_map(
        per_device,
        mesh=mesh,
        in_specs=placed,
        out_specs=(P(("seq", "exp"), None, None), P("exp", "seq", None)),
        check_vma=False,
    )
```

```python
import functools

import jax
import jax.numpy as jnp
from jax import lax
from jax.experimental import pallas as pl
from jax.experimental.pallas import tpu as pltpu
from jax.sharding import PartitionSpec as P

MESH = pl.DeviceIdType.MESH
BF = jnp.bfloat16
F32 = jnp.float32
SIDE = 4
CHIPS = 16
BLOCKS = SIDE * SIDE
SHARE = 16
LC = 128
HS = 128
SLOTS = 32
PARTS = 3
EXTRA = 128
PARENT = {
    1: 0, 3: 0, 6: 3, 2: 3, 4: 3, 5: 6, 7: 6, 8: 6,
    -1: 0, -3: 0, -6: -3, -2: -3, -4: -3, -5: -6, -7: -6,
}
OFFS = list(PARENT)
CHILDREN = {p: [o for o in OFFS if PARENT[o] == p] for p in set(PARENT.values())}
LEAVES = [o for o in OFFS if o not in CHILDREN]
RELAYS = [o for o in OFFS if o in CHILDREN]


def depth_of(o):
    return 0 if o == 0 else 1 + depth_of(PARENT[o])


DEPTH = max(depth_of(o) for o in RELAYS)
REACH = sorted({PARENT[o] - o for o in OFFS} | {o - PARENT[o] for o in OFFS})


def dot(a, b, dims):
    return lax.dot_general(a, b, (dims, ((), ())), preferred_element_type=F32)


NN = ((1,), (0,))
NT = ((1,), (1,))
TN = ((0,), (0,))


def split(a):
    hi = a.astype(BF)
    return hi, (a - hi.astype(F32)).astype(BF)


def remote(src, dst, send, recv, peer):
    return pltpu.make_async_remote_copy(
        src, dst, send, recv, device_id=peer, device_id_type=MESH
    )


def kernel(
    q_hbm,
    k_hbm,
    v_hbm,
    ld_hbm,
    hg_hbm,
    res_hbm,
    outp_ref,
    ng_hbm,
    rt_hbm,
    wt_hbm,
    wg_ref,
    wu_ref,
    attn_ref,
    hid_ref,
    q_ref,
    k_ref,
    v_ref,
    ld_ref,
    hg_ref,
    ng_ref,
    rt_ref,
    wt_ref,
    out1,
    in1,
    out2,
    inc,
    inner,
    grow,
    att,
    w2,
    part,
    full,
    rsbuf,
    rly,
    resbuf,
    res16,
    mix,
    nrm,
    rts,
    wts,
    picks,
    slots,
    other,
    sw,
    wb,
    acc2,
    lsem,
    asend,
    arecv,
    xsend,
    xrecv,
    bsend,
    brecv,
    zsend,
    zrecv,
    gsend,
    grecv,
    psend,
    precv,
    ssend,
    srecv,
):
    s = lax.axis_index("seq")
    e = lax.axis_index("exp")
    x, y, z, c = s // SIDE, s % SIDE, e // 2, e % 2
    half = mix.shape[2]
    depth = 2 * half
    hidden = wg_ref.shape[1]

    drains = []

    def finish():
        for wait in drains:
            wait()

    def at(xx, yy, zz, cc):
        return (xx * SIDE + yy, zz * 2 + cc)

    sib = at(x, y, z, 1 - c)
    barrier = pltpu.get_barrier_semaphore()

    def greet(peer):
        pl.semaphore_signal(barrier, inc=1, device_id=peer, device_id_type=MESH)

    mine = pl.ds(pl.multiple_of(c * half, half), half)
    theirs = pl.ds(pl.multiple_of((1 - c) * half, half), half)
    own_k = pl.ds(pl.multiple_of(c * HS, HS), HS)
    w2_own = pltpu.make_async_copy(outp_ref.at[:, mine], w2.at[own_k, :], lsem.at[0])
    wg_copy = pltpu.make_async_copy(wg_ref.at[0], wb.at[pl.ds(0, hidden), :], lsem.at[1])
    wu_copy = pltpu.make_async_copy(wu_ref.at[0], wb.at[pl.ds(hidden, hidden), :], lsem.at[2])
    ins = [
        pltpu.make_async_copy(a, b, lsem.at[3 + i])
        for i, (a, b) in enumerate(
            (
                (ld_hbm, ld_ref),
                (k_hbm, k_ref),
                (v_hbm, v_ref),
                (q_hbm, q_ref),
                (rt_hbm, rt_ref),
                (wt_hbm, wt_ref),
                (hg_hbm, hg_ref),
                (ng_hbm, ng_ref),
                (res_hbm, resbuf.at[c]),
            )
        )
    ]
    for cp in ins:
        cp.start()
    w2_own.start()
    wg_copy.start()
    wu_copy.start()
    greet(sib)

    def greet_xy(d, _):
        greet(((s + d) % BLOCKS, e))
        return 0

    lax.fori_loop(1, BLOCKS, greet_xy, 0)
    for d in REACH:
        greet(at(x, y, (z + d) % CHIPS, c))

    for cp in ins[:3]:
        cp.wait()

    ti = lax.broadcasted_iota(jnp.int32, (LC, LC), 0)
    ji = lax.broadcasted_iota(jnp.int32, (LC, LC), 1)
    causal = ji <= ti
    run_cols, run_rows = [], []
    for b in range(2):
        lb = jnp.broadcast_to(ld_ref[b], (LC, LC))
        rc = jnp.sum(jnp.where(causal, lb, 0.0), axis=1, keepdims=True)
        rr = jnp.sum(jnp.where(ji == ti, rc, 0.0), axis=0, keepdims=True)
        run_cols.append(rc)
        run_rows.append(rr)
        total = rr[:, LC - 1 :]
        kw = k_ref[b].astype(F32) * jnp.exp(total - rc)
        hi, lo = split(kw)
        vb = v_ref[b]
        fresh = dot(hi, vb, TN) + dot(lo, vb, TN)
        lines = jnp.broadcast_to(total, (8, HS))
        for i in range(HS // SHARE):
            j = b * (HS // SHARE) + i
            out1[j, pl.ds(0, SHARE), :] = fresh[i * SHARE : (i + 1) * SHARE]
            out1[j, pl.ds(SHARE, 8), :] = lines

    pl.semaphore_wait(barrier, BLOCKS + len(REACH))

    def order(i):
        return BLOCKS // 2 + ((i + 1) // 2) * (1 - 2 * (i % 2))

    def first(j):
        return remote(out1.at[j], in1.at[s], asend.at[j], arecv.at[s], (j, e))

    def second(j):
        return remote(out2.at[j], inc.at[s], xsend.at[j], xrecv.at[s], (j, e))

    def loop(body, start=1):
        def turn(i, _):
            body((s + (order(i) if start == 0 else i)) % BLOCKS)
            return 0

        lax.fori_loop(start, BLOCKS - 1 + start, turn, 0)

    loop(lambda j: first(j).start(), 0)
    drains.append(lambda: loop(lambda j: first(j).wait_send()))
    in1[s] = out1[s]
    w2_sib = remote(outp_ref.at[:, theirs], w2.at[own_k, :], bsend.at[0], brecv.at[0], sib)
    w2_sib.start()
    drains.append(w2_sib.wait_send)
    res_sib = remote(res_hbm, resbuf.at[c], bsend.at[1], brecv.at[1], sib)
    res_sib.start()
    drains.append(res_sib.wait_send)
    for cp in ins[3:]:
        cp.wait()

    for b in range(2):
        rc, rr = run_cols[b], run_rows[b]
        decay = jnp.where(causal, jnp.exp(jnp.where(causal, rc - rr, 0.0)), 0.0)
        hi, lo = split(dot(q_ref[b], k_ref[b], NT) * decay)
        vb = v_ref[b]
        inner[b] = dot(hi, vb, NN) + dot(lo, vb, NN)
        grow[b] = jnp.broadcast_to(jnp.exp(rc), (LC, HS))

    loop(lambda j: remote(in1.at[j], in1.at[j], asend.at[j], arecv.at[j], (j, e)).wait_recv())
    run = jnp.zeros((SHARE, HS), F32)
    for j in range(BLOCKS):
        out2[j] = run
        keep = jnp.exp(in1[j, pl.ds(SHARE, 8), :])
        run = jnp.concatenate([keep] * (SHARE // 8), axis=0) * run + in1[j, pl.ds(0, SHARE), :]
    loop(lambda j: second(j).start(), 0)
    drains.append(lambda: loop(lambda j: second(j).wait_send()))
    inc[s] = out2[s]

    for b in range(2):
        for kk in range(2):
            for blk in range(CHIPS):
                cols = pl.ds(blk * LC, LC)
                rts[b * 2 + kk, pl.ds(blk, 1), :] = rt_ref[b, pl.ds(kk, 1), cols]
                wts[b * 2 + kk, pl.ds(blk, 1), :] = wt_ref[b, pl.ds(kk, 1), cols]
    before = (ti < ji).astype(F32).astype(BF)
    slot_id = lax.broadcasted_iota(jnp.int32, (SLOTS, LC), 0).astype(F32)
    ri = lax.broadcasted_iota(jnp.int32, (2 * LC, 2 * LC), 0)
    ci = lax.broadcasted_iota(jnp.int32, (2 * LC, 2 * LC), 1)
    rb, rtm = ri // LC, ri % LC
    perm = (ci == (rtm // 8) * 16 + rb * 8 + rtm % 8).astype(F32).astype(BF)

    def places(h0, h1):
        first = dot((h0 + h1).astype(BF), before, NN)
        return first, first + h0

    for ex in range(2):
        hits = []
        for b in range(2):
            r0 = rts[b * 2, pl.ds(s, 1), :]
            r1 = rts[b * 2 + 1, pl.ds(s, 1), :]
            hit = ((r0 == z * 2 + ex) | (r1 == z * 2 + ex)).astype(F32)
            hits.append(jnp.broadcast_to(hit, (8, LC)))
        p0, p1 = places(hits[0], hits[1])
        table = []
        for hh, pp in ((hits[0], p0), (hits[1], p1)):
            one = jnp.where(slot_id == pp[0:1, :], hh[0:1, :], 0.0)
            table.append(one)
        table = jnp.concatenate(table, axis=1).astype(BF)
        picks[pl.ds(ex * SLOTS, SLOTS), :] = dot(table, perm, NN).astype(BF)

    hits = [((rts[b * 2] == e) | (rts[b * 2 + 1] == e)).astype(F32) for b in range(2)]
    tws = [
        jnp.where(rts[b * 2] == e, wts[b * 2], 0.0)
        + jnp.where(rts[b * 2 + 1] == e, wts[b * 2 + 1], 0.0)
        for b in range(2)
    ]
    ranks = places(hits[0], hits[1])
    for blk in range(CHIPS):
        acc = jnp.zeros((8, SLOTS), F32)
        for b in range(2):
            row = slice(blk, blk + 1)
            one = jnp.where(slot_id == ranks[b][row], hits[b][row], 0.0).astype(BF)
            w = jnp.broadcast_to(tws[b][row], (8, LC))
            hi = w.astype(BF)
            rest = w - hi.astype(F32)
            mid, low = split(rest)
            acc = acc + (dot(hi, one, NT) + (dot(mid, one, NT) + dot(low, one, NT)))
        sw[:, pl.ds(blk * SLOTS, SLOTS)] = acc

    loop(lambda j: remote(inc.at[j], inc.at[j], xsend.at[j], xrecv.at[j], (j, e)).wait_recv())
    heads = []
    for b in range(2):
        state = inc[pl.ds(b * (HS // SHARE), HS // SHARE)].reshape(HS, HS)
        hi, lo = split(state)
        qb = q_ref[b]
        raw = inner[b] + grow[b] * (dot(qb, hi, NN) + dot(qb, lo, NN))
        meansq = jnp.mean(raw * raw, axis=1, keepdims=True)
        heads.append((raw * lax.rsqrt(meansq + 1e-06) * hg_ref[...]).reshape(CHIPS, 1, 8, HS))
    att[:, own_k] = jnp.concatenate(heads, axis=1).reshape(2 * LC, HS).astype(BF)
    att_sib = remote(att.at[:, own_k], att.at[:, own_k], bsend.at[2], brecv.at[2], sib)
    att_sib.start()
    drains.append(att_sib.wait_send)

    w2_own.wait()
    other_k = pl.ds(pl.multiple_of((1 - c) * HS, HS), HS)
    remote(outp_ref.at[:, theirs], w2.at[other_k, :], bsend.at[0], brecv.at[0], sib).wait_recv()
    remote(att.at[:, own_k], att.at[:, other_k], bsend.at[2], brecv.at[2], sib).wait_recv()
    width = half // PARTS

    def rows_of(zz):
        return pl.ds(pl.multiple_of((zz % CHIPS) * 16, 16), 16)

    def span(p):
        return pl.ds(p * width, width + (EXTRA if p == PARTS - 1 else 0))

    def send(cp):
        cp.start()
        drains.append(cp.wait_send)

    own_rows = rows_of(z)

    def rs_copy(o, p, src):
        i = OFFS.index(o)
        peer = at(x, y, (z - o + PARENT[o]) % CHIPS, c)
        dst = rsbuf.at[i, :, pl.ds(p * width, width)]
        return remote(src, dst, zsend.at[i, p], zrecv.at[i, p], peer)

    def rs_arrived(o, p):
        cols = pl.ds(p * width, width)
        i = OFFS.index(o)
        ref = rsbuf.at[i, :, cols]
        remote(ref, ref, zsend.at[i, p], zrecv.at[i, p], sib).wait_recv()
        return rsbuf[i, :, cols].astype(F32)

    def project(p):
        cols = pl.ds(p * width, width)
        got = dot(att[...], w2[:, cols], NN)
        full[:, cols] = got
        part[:, cols] = got.astype(BF)

    def leaves(level, p):
        cols = pl.ds(p * width, width)
        for o in LEAVES:
            if depth_of(o) == level:
                send(rs_copy(o, p, part.at[rows_of(z - o), cols]))

    def relay(level, p):
        cols = pl.ds(p * width, width)
        for o in RELAYS:
            if depth_of(o) != level:
                continue
            acc = full[rows_of(z - o), cols]
            for ch in CHILDREN[o]:
                acc = acc + rs_arrived(ch, p)
            r = RELAYS.index(o)
            rly[r, :, cols] = acc.astype(BF)
            send(rs_copy(o, p, rly.at[r, :, cols]))

    def ag_copy(o, p, src_z, peer):
        i = OFFS.index(o)
        ref = nrm.at[rows_of(src_z), span(p)]
        return remote(ref, ref, gsend.at[i, p], grecv.at[i, p], peer)

    def total(p):
        cols = pl.ds(p * width, width)
        acc = full[own_rows, cols] + res16[:, cols]
        for ch in CHILDREN[0]:
            acc = acc + rs_arrived(ch, p)
        mix[c, :, cols] = acc
        gain = ng_ref[:, pl.ds(pl.multiple_of(c * half + p * width, 128), width)]
        nrm[own_rows, cols] = (acc * gain).astype(BF)
        if p == PARTS - 1:
            mix_sib = remote(mix.at[c], mix.at[c], bsend.at[3], brecv.at[3], sib)
            send(mix_sib)
            near = mix[c]
            ss = jnp.sum(near * near, axis=1, keepdims=True)
            remote(mix.at[c], mix.at[1 - c], bsend.at[3], brecv.at[3], sib).wait_recv()
            far = mix[1 - c]
            ss = ss + jnp.sum(far * far, axis=1, keepdims=True)
            scale = lax.rsqrt(ss * (1.0 / depth) + 1e-06)
            hi = scale.astype(BF).astype(F32)
            mid = (scale - hi).astype(BF).astype(F32)
            low = scale - hi - mid
            lane = lax.broadcasted_iota(jnp.int32, (16, EXTRA), 1)
            extra = jnp.where(
                lane == 0, hi, jnp.where(lane == 1, mid, jnp.where(lane == 2, low, 0.0))
            )
            nrm[own_rows, pl.ds(half, EXTRA)] = extra.astype(BF)
        spread(0, RELAYS, p)

    def spread(level, which, p):
        for o in OFFS:
            src = z - PARENT[o]
            if depth_of(PARENT[o]) == level and o in which:
                send(ag_copy(o, p, src, at(x, y, (src + o) % CHIPS, c)))

    def forward(level, p):
        for o in RELAYS:
            if depth_of(o) == level:
                ag_copy(o, p, z - o, sib).wait_recv()
        spread(level, RELAYS, p)

    def pick(p):
        for o in LEAVES:
            ag_copy(o, p, z - o, sib).wait_recv()
        cols = span(p)
        got = dot(picks[...], nrm[:, cols], NN).astype(BF)
        other[:, cols] = jnp.where(c == 0, got[SLOTS:], got[:SLOTS])
        send(
            remote(
                other.at[:, cols], slots.at[c, x, y, :, cols], psend.at[p], precv.at[p], sib
            )
        )
        slots[c, x, y, :, cols] = jnp.where(c == 0, got[:SLOTS], got[SLOTS:])

    def parts_of(p):
        size = width + (EXTRA if p == PARTS - 1 else 0)
        left = size // 256 * 128
        return pl.ds(p * width, left), pl.ds(p * width + left, size - left)

    def step1(h, d):
        dx, dy = (d, 0) if h == 0 else (0, d)
        return (x + dx) % SIDE, (y + dy) % SIDE

    def step2(h, d):
        dx, dy = (0, d) if h == 0 else (d, 0)
        return (x + dx) % SIDE, (y + dy) % SIDE

    def one(h, where, cols):
        return slots.at[h, where[0], where[1], :, cols]

    def four(h, where, cols):
        if h == 0:
            return slots.at[h, :, where[1], :, cols]
        return slots.at[h, where[0], :, :, cols]

    def xy(h, p, stage, i, ref, where):
        return remote(
            ref, ref, ssend.at[h, p, stage, i], srecv.at[h, p, stage, i], at(*where, z, c)
        )

    def hop1(p):
        cols = span(p)
        remote(
            other.at[:, cols], slots.at[1 - c, x, y, :, cols], psend.at[p], precv.at[p], sib
        ).wait_recv()
        for h in range(2):
            for i, d in reversed(list(enumerate((1, -1, 2)))):
                send(xy(h, p, 0, i, one(h, (x, y), cols), step1(h, d)))

    def hop3(p):
        for h in range(2):
            for i, d in enumerate((1, -1, 2)):
                back = step1(h, -d)
                xy(h, p, 0, i, one(h, back, span(p)), back).wait_recv()
            for i, d in enumerate((1, -1)):
                send(xy(h, p, 2, i, four(h, (x, y), span(p)), step2(h, d)))

    def hop4(p):
        for h in range(2):
            for i, d in enumerate((1, -1)):
                back = step2(h, -d)
                xy(h, p, 2, i, four(h, back, span(p)), back).wait_recv()
                send(xy(h, p, 3, i, four(h, back, parts_of(p)[i]), step2(h, d)))

    def multiply(p):
        for h in range(2):
            for i in range(2):
                far = step2(h, 2)
                xy(h, p, 3, i, four(h, far, parts_of(p)[i]), far).wait_recv()
        if p == 0:
            wg_copy.wait()
            wu_copy.wait()
        for n in range(2):
            rows = pl.ds(n * 256, 256)
            got = None
            for h in range(2):
                rhs = slots[h, pl.ds(2 * n, 2), :, :, pl.ds(p * width, width)]
                rhs = rhs.reshape(256, width)
                term = dot(wb[:, pl.ds(h * half + p * width, width)], rhs, NT)
                got = term if got is None else got + term
            acc2[:, rows] = got if p == 0 else acc2[:, rows] + got

    remote(res_hbm, resbuf.at[1 - c], bsend.at[1], brecv.at[1], sib).wait_recv()
    for cc in range(2):
        for i in range(4):
            two = resbuf[cc, i, :, mine].astype(F32)
            for b in range(2):
                res16[pl.ds(b * 8 + cc * 4 + i, 1), :] = two[b : b + 1, :]
    def each(*steps):
        for p in range(PARTS):
            for step in steps:
                step(p)

    def leaf(level):
        return functools.partial(leaves, level)

    def near(level):
        return functools.partial(spread, level, LEAVES)

    each(project, leaf(DEPTH + 1))
    for level in range(DEPTH, 0, -1):
        each(leaf(level))
        each(functools.partial(relay, level))
    each(total, near(0))
    for level in range(1, DEPTH + 1):
        each(functools.partial(forward, level), near(level))
    pick(0)
    for p in range(1, PARTS):
        pick(p)
        hop1(p - 1)
    hop1(PARTS - 1)
    each(hop3)
    each(hop4)
    each(multiply)

    for h in range(2):
        for b in range(2):
            for i in range(4):
                attn_ref[i, pl.ds(b, 1), pl.ds(h * half, half)] = mix[
                    h, pl.ds(b * 8 + c * 4 + i, 1), :
                ]
    lane = lax.broadcasted_iota(jnp.int32, (8, EXTRA), 1)
    ones = jnp.where(lane < 3, 1.0, 0.0).astype(BF)
    for n in range(2):
        rows = pl.ds(n * 256, 256)
        extra = slots[0, pl.ds(2 * n, 2), :, :, pl.ds(half, EXTRA)].reshape(256, EXTRA)
        scale = dot(ones, extra, NT)[0:1, :]
        gate = acc2[pl.ds(0, hidden), rows] * scale
        hid_ref[0, :, rows] = (sw[0:1, rows] * scale) * (
            gate / (1.0 + jnp.exp(-gate)) * acc2[pl.ds(hidden, hidden), rows]
        )
    finish()


def per_device(
    residual,
    queries,
    key_vecs,
    value_vecs,
    log_decay,
    head_gain,
    out_proj,
    norm_gain,
    routes,
    route_weight,
    w_gate,
    w_up,
):
    model_width = residual.shape[2]
    half = model_width // 2
    hidden = w_gate.shape[1]
    vmem = pl.BlockSpec(memory_space=pltpu.VMEM)
    hbm = pl.BlockSpec(memory_space=pltpu.HBM)
    dma = pltpu.SemaphoreType.DMA
    spans = CHIPS * SLOTS
    return pl.pallas_call(
        kernel,
        out_shape=(
            jax.ShapeDtypeStruct(residual.shape, F32),
            jax.ShapeDtypeStruct((1, hidden, spans), F32),
        ),
        in_specs=[hbm] * 12,
        out_specs=(vmem, vmem),
        scratch_shapes=[
            pltpu.VMEM(queries.shape, BF),
            pltpu.VMEM(queries.shape, BF),
            pltpu.VMEM(queries.shape, BF),
            pltpu.VMEM(log_decay.shape, F32),
            pltpu.VMEM((1, HS), F32),
            pltpu.VMEM((1, model_width), F32),
            pltpu.VMEM((2, 2, CHIPS * LC), jnp.int32),
            pltpu.VMEM((2, 2, CHIPS * LC), F32),
            pltpu.VMEM((BLOCKS, SHARE + 8, HS), F32),
            pltpu.VMEM((BLOCKS, SHARE + 8, HS), F32),
            pltpu.VMEM((BLOCKS, SHARE, HS), F32),
            pltpu.VMEM((BLOCKS, SHARE, HS), F32),
            pltpu.VMEM((2, LC, HS), F32),
            pltpu.VMEM((2, LC, HS), F32),
            pltpu.VMEM((2 * LC, 2 * HS), BF),
            pltpu.VMEM((2 * HS, half), BF),
            pltpu.VMEM((2 * LC, half), BF),
            pltpu.VMEM((2 * LC, half), F32),
            pltpu.VMEM((len(OFFS), 16, half), BF),
            pltpu.VMEM((len(RELAYS), 16, half), BF),
            pltpu.VMEM((2,) + residual.shape, BF),
            pltpu.VMEM((16, half), F32),
            pltpu.VMEM((2, 16, half), F32),
            pltpu.VMEM((2 * LC, half + EXTRA), BF),
            pltpu.VMEM((4, CHIPS, LC), jnp.int32),
            pltpu.VMEM((4, CHIPS, LC), F32),
            pltpu.VMEM((2 * SLOTS, 2 * LC), BF),
            pltpu.VMEM((2, SIDE, SIDE, SLOTS, half + EXTRA), BF),
            pltpu.VMEM((SLOTS, half + EXTRA), BF),
            pltpu.VMEM((8, spans), F32),
            pltpu.VMEM((2 * hidden, model_width), BF),
            pltpu.VMEM((2 * hidden, spans), F32),
            dma((12,)),
            dma((BLOCKS,)),
            dma((BLOCKS,)),
            dma((BLOCKS,)),
            dma((BLOCKS,)),
            dma((5,)),
            dma((5,)),
            dma((len(OFFS), PARTS)),
            dma((len(OFFS), PARTS)),
            dma((len(OFFS), PARTS)),
            dma((len(OFFS), PARTS)),
            dma((PARTS,)),
            dma((PARTS,)),
            dma((2, PARTS, 4, 3)),
            dma((2, PARTS, 4, 3)),
        ],
        compiler_params=pltpu.CompilerParams(
            collective_id=0, has_side_effects=True, vmem_limit_bytes=48 << 20
        ),
        name="layer",
    )(*[pltpu.with_memory_space_constraint(a, pltpu.HBM) for a in (
        queries,
        key_vecs,
        value_vecs,
        log_decay,
        head_gain.reshape(1, -1),
        residual,
        out_proj,
        norm_gain.reshape(1, -1),
        jnp.transpose(routes, (1, 2, 0)),
        jnp.transpose(route_weight, (1, 2, 0)),
        w_gate,
        w_up,
    )])


def solution(mesh):
    placed = (
        P(("seq", "exp"), None, None),
        P(None, "seq", "exp"),
        P(None, "seq", "exp"),
        P(None, "seq", "exp"),
        P(None, "exp", "seq"),
        P("exp"),
        P("exp", None),
        P(),
        P(),
        P(),
        P("exp", "seq", None),
        P("exp", "seq", None),
    )
    return jax.shard_map(
        per_device,
        mesh=mesh,
        in_specs=placed,
        out_specs=(P(("seq", "exp"), None, None), P("exp", "seq", None)),
        check_vma=False,
    )
```

```python
import functools

import jax
import jax.numpy as jnp
from jax import lax
from jax.experimental import pallas as pl
from jax.experimental.pallas import tpu as pltpu
from jax.sharding import PartitionSpec as P

MESH = pl.DeviceIdType.MESH
BF = jnp.bfloat16
F32 = jnp.float32
SIDE = 4
CHIPS = 16
BLOCKS = SIDE * SIDE
SHARE = 16
LC = 128
HS = 128
SLOTS = 32
PARTS = 3
EXTRA = 128
PARENT = {
    1: 0, 3: 0, 6: 3, 2: 3, 4: 3, 5: 6, 7: 6, 8: 6,
    -1: 0, -2: 0, -5: -2, -3: -2, -4: -5, -6: -5, -7: -5,
}
OFFS = list(PARENT)
CHILDREN = {p: [o for o in OFFS if PARENT[o] == p] for p in set(PARENT.values())}
LEAVES = [o for o in OFFS if o not in CHILDREN]
RELAYS = [o for o in OFFS if o in CHILDREN]


def depth_of(o):
    return 0 if o == 0 else 1 + depth_of(PARENT[o])


DEPTH = max(depth_of(o) for o in RELAYS)
REACH = sorted({PARENT[o] - o for o in OFFS} | {o - PARENT[o] for o in OFFS})


def dot(a, b, dims):
    return lax.dot_general(a, b, (dims, ((), ())), preferred_element_type=F32)


NN = ((1,), (0,))
NT = ((1,), (1,))
TN = ((0,), (0,))


def split(a):
    hi = a.astype(BF)
    return hi, (a - hi.astype(F32)).astype(BF)


def remote(src, dst, send, recv, peer):
    return pltpu.make_async_remote_copy(
        src, dst, send, recv, device_id=peer, device_id_type=MESH
    )


def kernel(
    q_hbm,
    k_hbm,
    v_hbm,
    ld_hbm,
    hg_hbm,
    res_hbm,
    outp_ref,
    ng_hbm,
    rt_hbm,
    wt_hbm,
    wg_ref,
    wu_ref,
    attn_ref,
    hid_ref,
    q_ref,
    k_ref,
    v_ref,
    ld_ref,
    hg_ref,
    ng_ref,
    rt_ref,
    wt_ref,
    out1,
    in1,
    out2,
    inc,
    inner,
    grow,
    att,
    w2,
    part,
    full,
    rsbuf,
    rly,
    resbuf,
    res16,
    mix,
    nrm,
    rts,
    wts,
    picks,
    slots,
    other,
    sw,
    wb,
    acc2,
    lsem,
    asend,
    arecv,
    xsend,
    xrecv,
    bsend,
    brecv,
    zsend,
    zrecv,
    gsend,
    grecv,
    psend,
    precv,
    ssend,
    srecv,
):
    s = lax.axis_index("seq")
    e = lax.axis_index("exp")
    x, y, z, c = s // SIDE, s % SIDE, e // 2, e % 2
    half = mix.shape[2]
    depth = 2 * half
    hidden = wg_ref.shape[1]

    drains = []

    def finish():
        for wait in drains:
            wait()

    def at(xx, yy, zz, cc):
        return (xx * SIDE + yy, zz * 2 + cc)

    sib = at(x, y, z, 1 - c)
    barrier = pltpu.get_barrier_semaphore()

    def greet(peer):
        pl.semaphore_signal(barrier, inc=1, device_id=peer, device_id_type=MESH)

    mine = pl.ds(pl.multiple_of(c * half, half), half)
    theirs = pl.ds(pl.multiple_of((1 - c) * half, half), half)
    own_k = pl.ds(pl.multiple_of(c * HS, HS), HS)
    w2_own = pltpu.make_async_copy(outp_ref.at[:, mine], w2.at[own_k, :], lsem.at[0])
    wg_copy = pltpu.make_async_copy(wg_ref.at[0], wb.at[pl.ds(0, hidden), :], lsem.at[1])
    wu_copy = pltpu.make_async_copy(wu_ref.at[0], wb.at[pl.ds(hidden, hidden), :], lsem.at[2])
    ins = [
        pltpu.make_async_copy(a, b, lsem.at[3 + i])
        for i, (a, b) in enumerate(
            (
                (ld_hbm, ld_ref),
                (k_hbm, k_ref),
                (v_hbm, v_ref),
                (q_hbm, q_ref),
                (rt_hbm, rt_ref),
                (wt_hbm, wt_ref),
                (hg_hbm, hg_ref),
                (ng_hbm, ng_ref),
                (res_hbm, resbuf.at[c]),
            )
        )
    ]
    for cp in ins:
        cp.start()
    w2_own.start()
    wg_copy.start()
    wu_copy.start()
    greet(sib)

    def greet_xy(d, _):
        greet(((s + d) % BLOCKS, e))
        return 0

    lax.fori_loop(1, BLOCKS, greet_xy, 0)
    for d in REACH:
        greet(at(x, y, (z + d) % CHIPS, c))

    for cp in ins[:3]:
        cp.wait()

    ti = lax.broadcasted_iota(jnp.int32, (LC, LC), 0)
    ji = lax.broadcasted_iota(jnp.int32, (LC, LC), 1)
    causal = ji <= ti
    run_cols, run_rows = [], []
    for b in range(2):
        lb = jnp.broadcast_to(ld_ref[b], (LC, LC))
        rc = jnp.sum(jnp.where(causal, lb, 0.0), axis=1, keepdims=True)
        rr = jnp.sum(jnp.where(ji == ti, rc, 0.0), axis=0, keepdims=True)
        run_cols.append(rc)
        run_rows.append(rr)
        total = rr[:, LC - 1 :]
        kw = k_ref[b].astype(F32) * jnp.exp(total - rc)
        hi, lo = split(kw)
        vb = v_ref[b]
        fresh = dot(hi, vb, TN) + dot(lo, vb, TN)
        lines = jnp.broadcast_to(total, (8, HS))
        for i in range(HS // SHARE):
            j = b * (HS // SHARE) + i
            out1[j, pl.ds(0, SHARE), :] = fresh[i * SHARE : (i + 1) * SHARE]
            out1[j, pl.ds(SHARE, 8), :] = lines

    pl.semaphore_wait(barrier, BLOCKS + len(REACH))

    def order(i):
        return BLOCKS // 2 + ((i + 1) // 2) * (1 - 2 * (i % 2))

    def first(j):
        return remote(out1.at[j], in1.at[s], asend.at[j], arecv.at[s], (j, e))

    def second(j):
        return remote(out2.at[j], inc.at[s], xsend.at[j], xrecv.at[s], (j, e))

    def loop(body, start=1):
        def turn(i, _):
            body((s + (order(i) if start == 0 else i)) % BLOCKS)
            return 0

        lax.fori_loop(start, BLOCKS - 1 + start, turn, 0)

    loop(lambda j: first(j).start(), 0)
    drains.append(lambda: loop(lambda j: first(j).wait_send()))
    in1[s] = out1[s]
    w2_sib = remote(outp_ref.at[:, theirs], w2.at[own_k, :], bsend.at[0], brecv.at[0], sib)
    w2_sib.start()
    drains.append(w2_sib.wait_send)
    res_sib = remote(res_hbm, resbuf.at[c], bsend.at[1], brecv.at[1], sib)
    res_sib.start()
    drains.append(res_sib.wait_send)
    for cp in ins[3:]:
        cp.wait()

    for b in range(2):
        rc, rr = run_cols[b], run_rows[b]
        decay = jnp.where(causal, jnp.exp(jnp.where(causal, rc - rr, 0.0)), 0.0)
        hi, lo = split(dot(q_ref[b], k_ref[b], NT) * decay)
        vb = v_ref[b]
        inner[b] = dot(hi, vb, NN) + dot(lo, vb, NN)
        grow[b] = jnp.broadcast_to(jnp.exp(rc), (LC, HS))

    loop(lambda j: remote(in1.at[j], in1.at[j], asend.at[j], arecv.at[j], (j, e)).wait_recv())
    run = jnp.zeros((SHARE, HS), F32)
    for j in range(BLOCKS):
        out2[j] = run
        keep = jnp.exp(in1[j, pl.ds(SHARE, 8), :])
        run = jnp.concatenate([keep] * (SHARE // 8), axis=0) * run + in1[j, pl.ds(0, SHARE), :]
    loop(lambda j: second(j).start(), 0)
    drains.append(lambda: loop(lambda j: second(j).wait_send()))
    inc[s] = out2[s]

    for b in range(2):
        for kk in range(2):
            for blk in range(CHIPS):
                cols = pl.ds(blk * LC, LC)
                rts[b * 2 + kk, pl.ds(blk, 1), :] = rt_ref[b, pl.ds(kk, 1), cols]
                wts[b * 2 + kk, pl.ds(blk, 1), :] = wt_ref[b, pl.ds(kk, 1), cols]
    before = (ti < ji).astype(F32).astype(BF)
    slot_id = lax.broadcasted_iota(jnp.int32, (SLOTS, LC), 0).astype(F32)
    ri = lax.broadcasted_iota(jnp.int32, (2 * LC, 2 * LC), 0)
    ci = lax.broadcasted_iota(jnp.int32, (2 * LC, 2 * LC), 1)
    rb, rtm = ri // LC, ri % LC
    perm = (ci == (rtm // 8) * 16 + rb * 8 + rtm % 8).astype(F32).astype(BF)

    def places(h0, h1):
        first = dot((h0 + h1).astype(BF), before, NN)
        return first, first + h0

    for ex in range(2):
        hits = []
        for b in range(2):
            r0 = rts[b * 2, pl.ds(s, 1), :]
            r1 = rts[b * 2 + 1, pl.ds(s, 1), :]
            hit = ((r0 == z * 2 + ex) | (r1 == z * 2 + ex)).astype(F32)
            hits.append(jnp.broadcast_to(hit, (8, LC)))
        p0, p1 = places(hits[0], hits[1])
        table = []
        for hh, pp in ((hits[0], p0), (hits[1], p1)):
            one = jnp.where(slot_id == pp[0:1, :], hh[0:1, :], 0.0)
            table.append(one)
        table = jnp.concatenate(table, axis=1).astype(BF)
        picks[pl.ds(ex * SLOTS, SLOTS), :] = dot(table, perm, NN).astype(BF)

    hits = [((rts[b * 2] == e) | (rts[b * 2 + 1] == e)).astype(F32) for b in range(2)]
    tws = [
        jnp.where(rts[b * 2] == e, wts[b * 2], 0.0)
        + jnp.where(rts[b * 2 + 1] == e, wts[b * 2 + 1], 0.0)
        for b in range(2)
    ]
    ranks = places(hits[0], hits[1])
    for blk in range(CHIPS):
        acc = jnp.zeros((8, SLOTS), F32)
        for b in range(2):
            row = slice(blk, blk + 1)
            one = jnp.where(slot_id == ranks[b][row], hits[b][row], 0.0).astype(BF)
            w = jnp.broadcast_to(tws[b][row], (8, LC))
            hi = w.astype(BF)
            rest = w - hi.astype(F32)
            mid, low = split(rest)
            acc = acc + (dot(hi, one, NT) + (dot(mid, one, NT) + dot(low, one, NT)))
        sw[:, pl.ds(blk * SLOTS, SLOTS)] = acc

    loop(lambda j: remote(inc.at[j], inc.at[j], xsend.at[j], xrecv.at[j], (j, e)).wait_recv())
    heads = []
    for b in range(2):
        state = inc[pl.ds(b * (HS // SHARE), HS // SHARE)].reshape(HS, HS)
        hi, lo = split(state)
        qb = q_ref[b]
        raw = inner[b] + grow[b] * (dot(qb, hi, NN) + dot(qb, lo, NN))
        meansq = jnp.mean(raw * raw, axis=1, keepdims=True)
        heads.append((raw * lax.rsqrt(meansq + 1e-06) * hg_ref[...]).reshape(CHIPS, 1, 8, HS))
    att[:, own_k] = jnp.concatenate(heads, axis=1).reshape(2 * LC, HS).astype(BF)
    att_sib = remote(att.at[:, own_k], att.at[:, own_k], bsend.at[2], brecv.at[2], sib)
    att_sib.start()
    drains.append(att_sib.wait_send)

    w2_own.wait()
    other_k = pl.ds(pl.multiple_of((1 - c) * HS, HS), HS)
    remote(outp_ref.at[:, theirs], w2.at[other_k, :], bsend.at[0], brecv.at[0], sib).wait_recv()
    remote(att.at[:, own_k], att.at[:, other_k], bsend.at[2], brecv.at[2], sib).wait_recv()
    width = half // PARTS

    def rows_of(zz):
        return pl.ds(pl.multiple_of((zz % CHIPS) * 16, 16), 16)

    def span(p):
        return pl.ds(p * width, width + (EXTRA if p == PARTS - 1 else 0))

    def send(cp):
        cp.start()
        drains.append(cp.wait_send)

    own_rows = rows_of(z)

    def rs_copy(o, p, src):
        i = OFFS.index(o)
        peer = at(x, y, (z - o + PARENT[o]) % CHIPS, c)
        dst = rsbuf.at[i, :, pl.ds(p * width, width)]
        return remote(src, dst, zsend.at[i, p], zrecv.at[i, p], peer)

    def rs_arrived(o, p):
        cols = pl.ds(p * width, width)
        i = OFFS.index(o)
        ref = rsbuf.at[i, :, cols]
        remote(ref, ref, zsend.at[i, p], zrecv.at[i, p], sib).wait_recv()
        return rsbuf[i, :, cols].astype(F32)

    def project(p):
        cols = pl.ds(p * width, width)
        got = dot(att[...], w2[:, cols], NN)
        full[:, cols] = got
        part[:, cols] = got.astype(BF)

    def leaves(level, p):
        cols = pl.ds(p * width, width)
        for o in LEAVES:
            if depth_of(o) == level:
                send(rs_copy(o, p, part.at[rows_of(z - o), cols]))

    def relay(level, p):
        cols = pl.ds(p * width, width)
        for o in RELAYS:
            if depth_of(o) != level:
                continue
            acc = full[rows_of(z - o), cols]
            for ch in CHILDREN[o]:
                acc = acc + rs_arrived(ch, p)
            r = RELAYS.index(o)
            rly[r, :, cols] = acc.astype(BF)
            send(rs_copy(o, p, rly.at[r, :, cols]))

    def ag_copy(o, p, src_z, peer):
        i = OFFS.index(o)
        ref = nrm.at[rows_of(src_z), span(p)]
        return remote(ref, ref, gsend.at[i, p], grecv.at[i, p], peer)

    def total(p):
        cols = pl.ds(p * width, width)
        acc = full[own_rows, cols] + res16[:, cols]
        for ch in CHILDREN[0]:
            acc = acc + rs_arrived(ch, p)
        mix[c, :, cols] = acc
        gain = ng_ref[:, pl.ds(pl.multiple_of(c * half + p * width, 128), width)]
        nrm[own_rows, cols] = (acc * gain).astype(BF)
        if p == PARTS - 1:
            mix_sib = remote(mix.at[c], mix.at[c], bsend.at[3], brecv.at[3], sib)
            send(mix_sib)
            near = mix[c]
            ss = jnp.sum(near * near, axis=1, keepdims=True)
            remote(mix.at[c], mix.at[1 - c], bsend.at[3], brecv.at[3], sib).wait_recv()
            far = mix[1 - c]
            ss = ss + jnp.sum(far * far, axis=1, keepdims=True)
            scale = lax.rsqrt(ss * (1.0 / depth) + 1e-06)
            hi = scale.astype(BF).astype(F32)
            mid = (scale - hi).astype(BF).astype(F32)
            low = scale - hi - mid
            lane = lax.broadcasted_iota(jnp.int32, (16, EXTRA), 1)
            extra = jnp.where(
                lane == 0, hi, jnp.where(lane == 1, mid, jnp.where(lane == 2, low, 0.0))
            )
            nrm[own_rows, pl.ds(half, EXTRA)] = extra.astype(BF)
        spread(0, RELAYS, p)

    def spread(level, which, p):
        for o in OFFS:
            src = z - PARENT[o]
            if depth_of(PARENT[o]) == level and o in which:
                send(ag_copy(o, p, src, at(x, y, (src + o) % CHIPS, c)))

    def forward(level, p):
        for o in RELAYS:
            if depth_of(o) == level:
                ag_copy(o, p, z - o, sib).wait_recv()
        spread(level, RELAYS, p)

    def pick(p):
        for o in LEAVES:
            ag_copy(o, p, z - o, sib).wait_recv()
        cols = span(p)
        got = dot(picks[...], nrm[:, cols], NN).astype(BF)
        other[:, cols] = jnp.where(c == 0, got[SLOTS:], got[:SLOTS])
        send(
            remote(
                other.at[:, cols], slots.at[c, x, y, :, cols], psend.at[p], precv.at[p], sib
            )
        )
        slots[c, x, y, :, cols] = jnp.where(c == 0, got[:SLOTS], got[SLOTS:])

    def parts_of(p):
        size = width + (EXTRA if p == PARTS - 1 else 0)
        left = size // 256 * 128
        return pl.ds(p * width, left), pl.ds(p * width + left, size - left)

    def step1(h, d):
        dx, dy = (d, 0) if h == 0 else (0, d)
        return (x + dx) % SIDE, (y + dy) % SIDE

    def step2(h, d):
        dx, dy = (0, d) if h == 0 else (d, 0)
        return (x + dx) % SIDE, (y + dy) % SIDE

    def one(h, where, cols):
        return slots.at[h, where[0], where[1], :, cols]

    def four(h, where, cols):
        if h == 0:
            return slots.at[h, :, where[1], :, cols]
        return slots.at[h, where[0], :, :, cols]

    def xy(h, p, stage, i, ref, where):
        return remote(
            ref, ref, ssend.at[h, p, stage, i], srecv.at[h, p, stage, i], at(*where, z, c)
        )

    def hop1(p):
        cols = span(p)
        remote(
            other.at[:, cols], slots.at[1 - c, x, y, :, cols], psend.at[p], precv.at[p], sib
        ).wait_recv()
        for h in range(2):
            for i, d in reversed(list(enumerate((1, -1, 2)))):
                send(xy(h, p, 0, i, one(h, (x, y), cols), step1(h, d)))

    def hop3(p):
        for h in range(2):
            for i, d in enumerate((1, -1, 2)):
                back = step1(h, -d)
                xy(h, p, 0, i, one(h, back, span(p)), back).wait_recv()
            for i, d in enumerate((1, -1)):
                send(xy(h, p, 2, i, four(h, (x, y), span(p)), step2(h, d)))

    def hop4(p):
        for h in range(2):
            for i, d in enumerate((1, -1)):
                back = step2(h, -d)
                xy(h, p, 2, i, four(h, back, span(p)), back).wait_recv()
                send(xy(h, p, 3, i, four(h, back, parts_of(p)[i]), step2(h, d)))

    def multiply(p):
        for h in range(2):
            for i in range(2):
                far = step2(h, 2)
                xy(h, p, 3, i, four(h, far, parts_of(p)[i]), far).wait_recv()
        if p == 0:
            wg_copy.wait()
            wu_copy.wait()
        for n in range(2):
            rows = pl.ds(n * 256, 256)
            got = None
            for h in range(2):
                rhs = slots[h, pl.ds(2 * n, 2), :, :, pl.ds(p * width, width)]
                rhs = rhs.reshape(256, width)
                term = dot(wb[:, pl.ds(h * half + p * width, width)], rhs, NT)
                got = term if got is None else got + term
            acc2[:, rows] = got if p == 0 else acc2[:, rows] + got

    remote(res_hbm, resbuf.at[1 - c], bsend.at[1], brecv.at[1], sib).wait_recv()
    for cc in range(2):
        for i in range(4):
            two = resbuf[cc, i, :, mine].astype(F32)
            for b in range(2):
                res16[pl.ds(b * 8 + cc * 4 + i, 1), :] = two[b : b + 1, :]
    def each(*steps):
        for p in range(PARTS):
            for step in steps:
                step(p)

    def leaf(level):
        return functools.partial(leaves, level)

    def near(level):
        return functools.partial(spread, level, LEAVES)

    each(project, leaf(DEPTH + 1))
    for level in range(DEPTH, 0, -1):
        each(leaf(level))
        each(functools.partial(relay, level))
    each(total, near(0))
    for level in range(1, DEPTH + 1):
        each(functools.partial(forward, level), near(level))
    pick(0)
    for p in range(1, PARTS):
        pick(p)
        hop1(p - 1)
    hop1(PARTS - 1)
    each(hop3)
    each(hop4)
    each(multiply)

    for h in range(2):
        for b in range(2):
            for i in range(4):
                attn_ref[i, pl.ds(b, 1), pl.ds(h * half, half)] = mix[
                    h, pl.ds(b * 8 + c * 4 + i, 1), :
                ]
    lane = lax.broadcasted_iota(jnp.int32, (8, EXTRA), 1)
    ones = jnp.where(lane < 3, 1.0, 0.0).astype(BF)
    for n in range(2):
        rows = pl.ds(n * 256, 256)
        extra = slots[0, pl.ds(2 * n, 2), :, :, pl.ds(half, EXTRA)].reshape(256, EXTRA)
        scale = dot(ones, extra, NT)[0:1, :]
        gate = acc2[pl.ds(0, hidden), rows] * scale
        hid_ref[0, :, rows] = (sw[0:1, rows] * scale) * (
            gate / (1.0 + jnp.exp(-gate)) * acc2[pl.ds(hidden, hidden), rows]
        )
    finish()


def per_device(
    residual,
    queries,
    key_vecs,
    value_vecs,
    log_decay,
    head_gain,
    out_proj,
    norm_gain,
    routes,
    route_weight,
    w_gate,
    w_up,
):
    model_width = residual.shape[2]
    half = model_width // 2
    hidden = w_gate.shape[1]
    vmem = pl.BlockSpec(memory_space=pltpu.VMEM)
    hbm = pl.BlockSpec(memory_space=pltpu.HBM)
    dma = pltpu.SemaphoreType.DMA
    spans = CHIPS * SLOTS
    return pl.pallas_call(
        kernel,
        out_shape=(
            jax.ShapeDtypeStruct(residual.shape, F32),
            jax.ShapeDtypeStruct((1, hidden, spans), F32),
        ),
        in_specs=[hbm] * 12,
        out_specs=(vmem, vmem),
        scratch_shapes=[
            pltpu.VMEM(queries.shape, BF),
            pltpu.VMEM(queries.shape, BF),
            pltpu.VMEM(queries.shape, BF),
            pltpu.VMEM(log_decay.shape, F32),
            pltpu.VMEM((1, HS), F32),
            pltpu.VMEM((1, model_width), F32),
            pltpu.VMEM((2, 2, CHIPS * LC), jnp.int32),
            pltpu.VMEM((2, 2, CHIPS * LC), F32),
            pltpu.VMEM((BLOCKS, SHARE + 8, HS), F32),
            pltpu.VMEM((BLOCKS, SHARE + 8, HS), F32),
            pltpu.VMEM((BLOCKS, SHARE, HS), F32),
            pltpu.VMEM((BLOCKS, SHARE, HS), F32),
            pltpu.VMEM((2, LC, HS), F32),
            pltpu.VMEM((2, LC, HS), F32),
            pltpu.VMEM((2 * LC, 2 * HS), BF),
            pltpu.VMEM((2 * HS, half), BF),
            pltpu.VMEM((2 * LC, half), BF),
            pltpu.VMEM((2 * LC, half), F32),
            pltpu.VMEM((len(OFFS), 16, half), BF),
            pltpu.VMEM((len(RELAYS), 16, half), BF),
            pltpu.VMEM((2,) + residual.shape, BF),
            pltpu.VMEM((16, half), F32),
            pltpu.VMEM((2, 16, half), F32),
            pltpu.VMEM((2 * LC, half + EXTRA), BF),
            pltpu.VMEM((4, CHIPS, LC), jnp.int32),
            pltpu.VMEM((4, CHIPS, LC), F32),
            pltpu.VMEM((2 * SLOTS, 2 * LC), BF),
            pltpu.VMEM((2, SIDE, SIDE, SLOTS, half + EXTRA), BF),
            pltpu.VMEM((SLOTS, half + EXTRA), BF),
            pltpu.VMEM((8, spans), F32),
            pltpu.VMEM((2 * hidden, model_width), BF),
            pltpu.VMEM((2 * hidden, spans), F32),
            dma((12,)),
            dma((BLOCKS,)),
            dma((BLOCKS,)),
            dma((BLOCKS,)),
            dma((BLOCKS,)),
            dma((5,)),
            dma((5,)),
            dma((len(OFFS), PARTS)),
            dma((len(OFFS), PARTS)),
            dma((len(OFFS), PARTS)),
            dma((len(OFFS), PARTS)),
            dma((PARTS,)),
            dma((PARTS,)),
            dma((2, PARTS, 4, 3)),
            dma((2, PARTS, 4, 3)),
        ],
        compiler_params=pltpu.CompilerParams(
            collective_id=0, has_side_effects=True, vmem_limit_bytes=48 << 20
        ),
        name="layer",
    )(*[pltpu.with_memory_space_constraint(a, pltpu.HBM) for a in (
        queries,
        key_vecs,
        value_vecs,
        log_decay,
        head_gain.reshape(1, -1),
        residual,
        out_proj,
        norm_gain.reshape(1, -1),
        jnp.transpose(routes, (1, 2, 0)),
        jnp.transpose(route_weight, (1, 2, 0)),
        w_gate,
        w_up,
    )])


def solution(mesh):
    placed = (
        P(("seq", "exp"), None, None),
        P(None, "seq", "exp"),
        P(None, "seq", "exp"),
        P(None, "seq", "exp"),
        P(None, "exp", "seq"),
        P("exp"),
        P("exp", None),
        P(),
        P(),
        P(),
        P("exp", "seq", None),
        P("exp", "seq", None),
    )
    return jax.shard_map(
        per_device,
        mesh=mesh,
        in_specs=placed,
        out_specs=(P(("seq", "exp"), None, None), P("exp", "seq", None)),
        check_vma=False,
    )
```
